32 devices in a mesh: grp: 2 (over y), cls: 8 (over z, x), img: 2 (over core).
Axes of the slice: x: 2, y: 2, z: 4, core: 2. Of those that a mesh axis runs over, the one named last changes fastest.
Arguments:
- embeddings: bfloat16 [4096, 1536], P(('grp', 'img'), 'cls'), parts along dimension 0, may hold values from -6 to 6, as said below
- labels: int32 [4096], P(('grp', 'img')), parts along dimension 0, may hold values from 0 to 1023
- weights: float32 [3072, 1024], P(('grp', 'img'), 'cls'), parts along dimension 0, may hold values from -12 to 12, as said below
- strength: int32 [2], P('grp'), parts along dimension 0, may hold values from 0 to 3
Outputs:
- new_weights: float32 [3072, 1024], P(('grp', 'img'), 'cls'), parts along dimension 0
- losses: float32 [4096], P(('grp', 'img')), parts along dimension 0
The draws below stay inside these ranges and needn't reach their ends.
There are 2 independent parts, one for each index of `grp`. The reference program is written for one: setup_inputs(seed, part) draws one part's arguments, and reference() takes and returns one part's arrays. A program takes and returns all parts, laid end to end along the dimension named above; each array names one. Nothing has to cross between parts.
Inputs may be any that keep to these rules, and one draw needn't show every extreme that they name: embeddings of order one. Initial probe weights of order a few.
All inputs are finite; a program needn't handle non-finite values.
Results may differ from the reference program's by a relative error of at most 0.0032.
Values may be sent and summed in bfloat16 or wider, within the bound.
A program may use at most 64 MiB of HBM per device.

```python
import math
import jax
import jax.numpy as jnp
from jax import lax

D = 1536
ITERS = 2
CLASSES = 1024
IMAGES = 2048


def base_weights(key):
    return 3.0 * jax.random.truncated_normal(jax.random.fold_in(key, 11), -4.0, 4.0, (D, CLASSES), jnp.float32)


def draw_weights(key, part):
    values = base_weights(key)
    return values


def draw_embeddings(key, part):
    inner = jax.random.fold_in(key, 31)
    values = jax.random.truncated_normal(inner, -4.0, 4.0, (IMAGES, D), jnp.float32)
    return values.astype(jnp.bfloat16)


def touch_ends(result, rng, low, high):
    dims = result.shape
    place = [jax.random.randint(jax.random.fold_in(rng, axis), (), 0, dims[axis]) for axis in range(len(dims))]
    result = result.at[tuple(place)].set(low)
    longest = dims.index(max(dims))
    place[longest] = (place[longest] + 1) % dims[longest]
    return result.at[tuple(place)].set(high)


def setup_inputs(seed: int = 0, part: int = 0) -> dict:
    splits = jax.random.split(jax.random.key(seed), 5)
    part_keys = jax.random.split(jax.random.fold_in(splits[4], part), 5)
    return {
        "embeddings": draw_embeddings(jax.random.fold_in(jax.random.fold_in(splits[4], part), 71), part),
        "labels": touch_ends(jax.random.randint(part_keys[1], (IMAGES,), 0, CLASSES), jax.random.fold_in(part_keys[1], 1), 0, CLASSES - 1).astype(jnp.int32),
        "weights": draw_weights(jax.random.fold_in(jax.random.fold_in(splits[4], part), 71), part),
        "strength": jax.random.randint(part_keys[3], (1,), 0, 4).astype(jnp.int32),
    }


def reference(embeddings, labels, weights, strength):
    scale = 1.0 / math.sqrt(D)
    lam = 16.0 * 0.01 * jnp.exp2(strength[0].astype(jnp.float32))
    classes = lax.iota(jnp.int32, CLASSES)
    onehot = (labels[:, None] == classes[None, :]).astype(jnp.float32)
    master = weights
    losses = jnp.zeros((IMAGES,), jnp.float32)
    for step in range(ITERS):
        operand = master.astype(jnp.bfloat16)
        logits = jnp.dot(embeddings, operand, preferred_element_type=jnp.float32) * scale
        top = lax.optimization_barrier(jnp.max(logits, axis=1))
        total = lax.optimization_barrier(jnp.sum(jnp.exp(logits - top[:, None]), axis=1))
        lse = top + jnp.log(total)
        picked = lax.optimization_barrier(jnp.sum(logits * onehot, axis=1))
        losses = lse - picked
        resid = (jnp.exp(logits - lse[:, None]) - onehot).astype(jnp.bfloat16)
        grad = lax.dot_general(embeddings, resid, (((0,), (0,)), ((), ())), preferred_element_type=jnp.float32) * scale
        moved = master - 16.0 * grad
        master = jnp.sign(moved) * jnp.maximum(jnp.abs(moved) - lam, 0.0)
    return (master, losses)
```

```python
import functools
import math

import jax
import jax.numpy as jnp
from jax import lax
from jax.experimental import pallas as pl
from jax.experimental.pallas import tpu as pltpu
from jax.sharding import PartitionSpec as P

D = 1536
ITERS = 2
MESH = pl.DeviceIdType.MESH
SCALE = 1.0 / math.sqrt(D)

NX, NZ = 2, 4
N = NX * NZ
IMGS, WIDTH, CLS = 1024, 192, 128
HALF = WIDTH // 2
PAIR = 2 * CLS
FEATS = D // 2
CHUNK = 256
CHUNKS = IMGS // CHUNK
JOBS = FEATS // 256
X_OWN, Z_OWN, X_MID, X_FAR, Z_FAR, Z_NEXT, UP_OWN, UP_FWD, UP_END, ACROSS = range(10)
SPLITS = (((0, 3), (3, 1)), ((0, 2), (2, 2)))


def shrink(master, grad, lam):
    moved = master - 16.0 * grad
    return jnp.sign(moved) * jnp.maximum(jnp.abs(moved) - lam, 0.0)


def kernel(x_hbm, lab_ref, w_hbm, s_ref, out_ref, loss_ref,
           xd, master, wb, wb2, acc, ex, resid, gsend, gown, grecv, hi, lo, ret,
           lses, picks, lbuf, load, e_send, e_recv, w_send, w_recv, m_send, m_recv,
           g_send, g_recv, l_send, l_recv, r_send, r_recv):
    me = lax.axis_index("cls")
    img = lax.axis_index("img")
    grp = lax.axis_index("grp")
    z, x = me // NX, me % NX
    inner = jnp.logical_and(z > 0, z < NZ - 1)
    outer = jnp.logical_not(inner)
    zp = z + 1 - 2 * (z % 2)
    zo = NZ - 1 - z
    zf = NZ - 1 - zp
    mate = (grp, me, 1 - img)
    side = (grp, z * NX + 1 - x, img)
    near = (grp, zp * NX + x, img)
    over = (grp, zo * NX + x, img)
    diag = (grp, zo * NX + 1 - x, img)

    def rows(at, n):
        return pl.ds(pl.multiple_of(at, 16), n)

    loads = [
        pltpu.make_async_copy(x_hbm, xd.at[rows(me * WIDTH, WIDTH)], load.at[0]),
        pltpu.make_async_copy(w_hbm, master.at[:, pl.ds(0, CLS)], load.at[1]),
    ]
    for c in loads:
        c.start()
    barrier = pltpu.get_barrier_semaphore()
    for to in (side, near):
        pl.semaphore_signal(barrier, inc=1, device_id=to, device_id_type=MESH)

    @pl.when(inner)
    def _():
        for to in (mate, over, diag):
            pl.semaphore_signal(barrier, inc=1, device_id=to, device_id_type=MESH)

    pl.semaphore_wait(barrier, 2 + 3 * inner.astype(jnp.int32))

    def remote(src, dst, sems, to):
        send, recv, at = sems
        return pltpu.make_async_remote_copy(
            src_ref=src, dst_ref=dst, send_sem=send.at[at], recv_sem=recv.at[at],
            device_id=to, device_id_type=MESH)

    def piece(kind, k, sz, sx, at, n, to, own=False):
        cols = pl.ds(k * CHUNK, CHUNK)
        place = xd.at[rows((sz * NX + sx) * WIDTH + at, n), cols]
        src = x_hbm.at[pl.ds(at, n), cols] if own else place
        return remote(src, place, (e_send, e_recv, (kind, k)), to)

    def across(k, sx, own=False):
        at = (1 - k) * HALF
        place = xd.at[rows((z * NX + sx) * WIDTH + at, HALF)]
        src = x_hbm.at[pl.ds(at, HALF)] if own else place
        return remote(src, place, (e_send, e_recv, (ACROSS, k)), side)

    def weights_piece(buf, k):
        return remote(buf, buf, (w_send, w_recv, k), near)

    def mate_weights(buf, half, at, j, k):
        cols = pl.ds(256 * j, 256) if j is not None else slice(None)
        place = buf.at[half, at, cols]
        return remote(place, place, (m_send, m_recv, k), mate)

    def ret_piece(step, j):
        place = ret.at[step, pl.ds(256 * j, 256)]
        return remote(place, place, (r_send, r_recv, (step, j)), near)

    def loss_piece():
        return remote(lbuf, lbuf, (r_send, r_recv, (ITERS, 0)), near)

    lam = 0.16 * jnp.exp2(s_ref[...].astype(jnp.float32))

    def step_to(old, change):
        moved = old - change
        return moved - jnp.clip(moved, -lam, lam)

    @pl.when(outer)
    def _():
        for k in range(CHUNKS):
            piece(UP_OWN, k, z, x, 0, WIDTH, near, own=True).start()
        for k in range(2):
            across(k, x, own=True).start()
        loads[1].wait()
        w = master[:, :CLS]
        top = w.astype(jnp.bfloat16)
        hi[...] = top
        weights_piece(hi, 0).start()
        lo[...] = (w - top.astype(jnp.float32)).astype(jnp.bfloat16)
        for half, kind in ((0, UP_FWD), (1, UP_END)):
            across(half, 1 - x).wait_recv()
            for k in range(CHUNKS):
                piece(kind, k, z, 1 - x, (1 - half) * HALF, HALF, near).start()
        weights_piece(lo, 1).start()
        for j in range(JOBS):
            r = slice(256 * j, 256 * j + 256)
            ret_piece(0, j).wait_recv()
            master[r, :CLS] = step_to(master[r, :CLS], ret[0, r].astype(jnp.float32))
        loss_piece().wait_recv()
        loss_ref[...] = lbuf[...]
        for j in range(JOBS):
            r = slice(256 * j, 256 * j + 256)
            ret_piece(1, j).wait_recv()
            out_ref[r] = step_to(master[r, :CLS], ret[1, r].astype(jnp.float32))
        loads[0].wait()
        for k in range(CHUNKS):
            piece(UP_OWN, k, z, x, 0, WIDTH, near, own=True).wait_send()
            piece(UP_FWD, k, z, 1 - x, HALF, HALF, near).wait_send()
            piece(UP_END, k, z, 1 - x, 0, HALF, near).wait_send()
        for k in range(2):
            across(k, x, own=True).wait_send()
        weights_piece(hi, 0).wait_send()
        weights_piece(lo, 1).wait_send()

    @pl.when(inner)
    def _():
        def x_own(k, sx=x, own=True):
            return piece(X_OWN, k, z, sx, 0, WIDTH, side, own)

        def z_own(k, sz=z, own=True):
            return piece(Z_OWN, k, sz, x, 0, WIDTH, over, own)

        def x_mid(k, sx=x):
            return piece(X_MID, k, zo, sx, 0, WIDTH, side)

        def x_far(k, sx=x):
            return piece(X_FAR, k, zf, sx, 0, HALF, side)

        def z_far(k, sz=zp):
            return piece(Z_FAR, k, sz, x, 0, WIDTH, over)

        def z_next(k, sz=zp):
            return piece(Z_NEXT, k, sz, 1 - x, HALF, HALF, over)

        def up_own(k):
            return piece(UP_OWN, k, zp, x, 0, WIDTH, near)

        def up_fwd(k):
            return piece(UP_FWD, k, zp, 1 - x, HALF, HALF, near)

        def up_end(k):
            return piece(UP_END, k, zp, 1 - x, 0, HALF, near)

        OWN_ROWS, NEAR_ROWS = pl.ds(0, CLS), pl.ds(CLS, CLS)

        for k in range(CHUNKS):
            x_own(k).start()
            z_own(k).start()
        loads[1].wait()
        for j in range(JOBS):
            r = slice(256 * j, 256 * j + 256)
            wb[img, :CLS, r] = master[r, :CLS].T.astype(jnp.bfloat16)
        mate_weights(wb, img, OWN_ROWS, None, 0).start()
        for k in range(CHUNKS):
            z_own(k, zo, False).wait_recv()
            x_mid(k).start()
            up_own(k).wait_recv()
            z_far(k).start()
        weights_piece(hi, 0).wait_recv()
        for j in range(JOBS):
            r = slice(256 * j, 256 * j + 256)
            part = hi[r].astype(jnp.float32)
            master[r, CLS:] = part
            wb[img, CLS:, r] = part.T.astype(jnp.bfloat16)
        mate_weights(wb, img, NEAR_ROWS, None, 1).start()
        for k in range(CHUNKS):
            z_far(k, zf).wait_recv()
            x_far(k).start()
            up_fwd(k).wait_recv()
            z_next(k).start()
        loads[0].wait()
        for k in range(CHUNKS):
            x_own(k, 1 - x, False).wait_recv()
        mate_weights(wb, 1 - img, OWN_ROWS, None, 0).wait_recv()
        mate_weights(wb, 1 - img, NEAR_ROWS, None, 1).wait_recv()

        mine = (z - 1) * NX + x
        peers = ((side, (z - 1) * NX + 1 - x), (over, (zo - 1) * NX + x), (diag, (zo - 1) * NX + 1 - x))

        def stat_piece(step, p, i, where):
            buf = (lses, picks)[step]
            at, n = SPLITS[step][p]
            place = buf.at[where, :, pl.ds(at * CHUNK, n * CHUNK)]
            return remote(place, place, (l_send, l_recv, (step, p, i)), peers[i][0])

        def dot(a, b):
            return jnp.dot(a, b, preferred_element_type=jnp.float32)

        def hot(r):
            row = lax.broadcasted_iota(jnp.int32, (PAIR, CHUNK), 0)
            cls = row + jnp.where(row < CLS, me * CLS, (zp * NX + x) * CLS - CLS)
            return lab_ref[:, r] == cls

        def stats(step, k, logits, tops):
            r = slice(k * CHUNK, k * CHUNK + CHUNK)
            buf = (lses, picks)[step]
            top = jnp.max(logits, axis=0, keepdims=True)
            e = jnp.exp(logits - top)
            ex[:, r] = e
            buf[mine, 0:1, r] = top + jnp.log(jnp.sum(e, axis=0, keepdims=True))
            tops.append(top)
            if step == ITERS - 1:
                buf[mine, 1:2, r] = jnp.sum(jnp.where(hot(r), logits, 0.0), axis=0, keepdims=True)

        def send_stats(step, k):
            for p, (at, n) in enumerate(SPLITS[step]):
                if k == at + n - 1:
                    for i in range(3):
                        stat_piece(step, p, i, mine).start()

        def residual(step, p, tops):
            buf = (lses, picks)[step]
            for i in range(3):
                stat_piece(step, p, i, peers[i][1]).wait_recv()
            at, n = SPLITS[step][p]
            for k in range(at, at + n):
                r = slice(k * CHUNK, k * CHUNK + CHUNK)
                parts = [buf[m, 0:1, r] for m in range(4)]
                top = functools.reduce(jnp.maximum, parts)
                lse = top + jnp.log(sum(jnp.exp(v - top) for v in parts))
                if step == ITERS - 1:
                    loss = lse - sum(buf[m, 1:2, r] for m in range(4))
                    for i in range(0, CHUNK, 128):
                        row = (k * CHUNK + i) // 128
                        lbuf[row:row + 1, :] = loss[:, i:i + 128]
                prob = ex[:, r] * jnp.exp(tops[k] - lse)
                resid[:, r] = (prob - jnp.where(hot(r), 1.0, 0.0)).astype(jnp.bfloat16)

        def grad_part(half, j, p, step):
            at, n = SPLITS[step][p]
            c = slice(at * CHUNK, (at + n) * CHUNK)
            return lax.dot_general(
                xd[rows(half * FEATS + j * 256, 256), c], resid[:, c], (((1,), (1,)), ((), ())),
                preferred_element_type=jnp.float32)

        def grad_piece(step, j):
            return remote(gsend.at[step, j], grecv.at[step, j], (g_send, g_recv, (step, j)), mate)

        for step in range(ITERS):
            last = step == ITERS - 1
            tops = []
            for k in range(CHUNKS):
                r = slice(k * CHUNK, k * CHUNK + CHUNK)
                if step == 0:
                    up_end(k).wait_recv()
                    x_mid(k, 1 - x).wait_recv()
                    x_far(k, 1 - x).wait_recv()
                    z_next(k, zf).wait_recv()
                    logits = (dot(wb[0], xd[:FEATS, r]) + dot(wb[1], xd[FEATS:, r])) * SCALE
                else:
                    if k == 0:
                        for j in range(JOBS):
                            mate_weights(wb2, 1 - img, slice(None), j, 2 + j).wait_recv()
                    logits = (acc[:, r] + dot(wb2[1 - img], xd[rows((1 - img) * FEATS, FEATS), r])) * SCALE
                stats(step, k, logits, tops)
                send_stats(step, k)
            residual(step, 0, tops)
            for j in range(JOBS):
                gsend[step, j] = grad_part(1 - img, j, 0, step)
            for j in range(JOBS):
                gown[j] = grad_part(img, j, 0, step)
            residual(step, 1, tops)
            if last:
                loss_ref[...] = lbuf[...]
                loss_piece().start()
            for j in range(JOBS):
                gsend[step, j] += grad_part(1 - img, j, 1, step)
                grad_piece(step, j).start()
            if not last:
                weights_piece(lo, 1).wait_recv()
            for j in range(JOBS):
                r = slice(256 * j, 256 * j + 256)
                grad = gown[j] + grad_part(img, j, 1, step)
                grad_piece(step, j).wait_recv()
                change = (grad + grecv[step, j]) * (16.0 * SCALE)
                ret[step, r] = change[:, CLS:].astype(jnp.bfloat16)
                ret_piece(step, j).start()
                if last:
                    out_ref[r] = step_to(master[r, :CLS], change[:, :CLS])
                else:
                    own = step_to(master[r, :CLS], change[:, :CLS])
                    other = step_to(master[r, CLS:] + lo[r].astype(jnp.float32), change[:, CLS:])
                    master[r, :CLS] = own
                    wb2[img, :CLS, r] = own.T.astype(jnp.bfloat16)
                    wb2[img, CLS:, r] = other.T.astype(jnp.bfloat16)
                    mate_weights(wb2, img, slice(None), j, 2 + j).start()
            if not last:
                for k in range(CHUNKS):
                    r = slice(k * CHUNK, k * CHUNK + CHUNK)
                    acc[:, r] = dot(wb2[img], xd[rows(img * FEATS, FEATS), r])

        for k in range(CHUNKS):
            for c in (x_own(k), z_own(k), x_mid(k), x_far(k), z_far(k), z_next(k)):
                c.wait_send()
        mate_weights(wb, img, OWN_ROWS, None, 0).wait_send()
        mate_weights(wb, img, NEAR_ROWS, None, 1).wait_send()
        for j in range(JOBS):
            mate_weights(wb2, img, slice(None), j, 2 + j).wait_send()
        for step in range(ITERS):
            for j in range(JOBS):
                grad_piece(step, j).wait_send()
                ret_piece(step, j).wait_send()
            for p in range(2):
                for i in range(3):
                    stat_piece(step, p, i, mine).wait_send()
        loss_piece().wait_send()


def fused(embeddings, labels, weights, strength):
    vmem = pl.BlockSpec(memory_space=pltpu.VMEM)
    hbm = pl.BlockSpec(memory_space=pl.ANY)
    f32, bf16 = jnp.float32, jnp.bfloat16
    dma = pltpu.SemaphoreType.DMA
    new_weights, losses = pl.pallas_call(
        kernel,
        out_shape=(
            jax.ShapeDtypeStruct((FEATS, CLS), f32),
            jax.ShapeDtypeStruct((IMGS // 128, 128), f32),
        ),
        in_specs=[hbm, vmem, hbm, vmem],
        out_specs=(vmem, vmem),
        scratch_shapes=[
            pltpu.VMEM((D, IMGS), bf16),
            pltpu.VMEM((FEATS, PAIR), f32),
            pltpu.VMEM((2, PAIR, FEATS), bf16),
            pltpu.VMEM((2, PAIR, FEATS), bf16),
            pltpu.VMEM((PAIR, IMGS), f32),
            pltpu.VMEM((PAIR, IMGS), f32),
            pltpu.VMEM((PAIR, IMGS), bf16),
            pltpu.VMEM((ITERS, JOBS, 256, PAIR), f32),
            pltpu.VMEM((JOBS, 256, PAIR), f32),
            pltpu.VMEM((ITERS, JOBS, 256, PAIR), f32),
            pltpu.VMEM((FEATS, CLS), bf16),
            pltpu.VMEM((FEATS, CLS), bf16),
            pltpu.VMEM((ITERS, FEATS, CLS), bf16),
            pltpu.VMEM((4, 1, IMGS), f32),
            pltpu.VMEM((4, 2, IMGS), f32),
            pltpu.VMEM((IMGS // 128, 128), f32),
            dma((2,)),
            dma((10, CHUNKS)),
            dma((10, CHUNKS)),
            dma((2,)),
            dma((2,)),
            dma((2 + JOBS,)),
            dma((2 + JOBS,)),
            dma((ITERS, JOBS)),
            dma((ITERS, JOBS)),
            dma((ITERS, 2, 3)),
            dma((ITERS, 2, 3)),
            dma((ITERS + 1, JOBS)),
            dma((ITERS + 1, JOBS)),
        ],
        compiler_params=pltpu.CompilerParams(
            collective_id=0, has_side_effects=True, vmem_limit_bytes=60 * 1024 * 1024
        ),
    )(embeddings.T, labels.reshape(1, IMGS), weights, strength.reshape(1, 1))
    return new_weights, losses.reshape(IMGS)


def general(embeddings, labels, weights, strength):
    lam = 16.0 * 0.01 * jnp.exp2(strength[0].astype(jnp.float32))
    full_x = lax.all_gather(embeddings, "cls", axis=1, tiled=True)
    cls_width = weights.shape[1]
    first_class = lax.axis_index("cls") * cls_width
    classes = first_class + lax.iota(jnp.int32, cls_width)
    onehot = (labels[:, None] == classes[None, :]).astype(jnp.float32)
    master = lax.all_gather(weights, "img", axis=0, tiled=True)
    operand = master.astype(jnp.bfloat16)
    losses = jnp.zeros((labels.shape[0],), jnp.float32)
    for step in range(ITERS):
        logits = jnp.dot(full_x, operand, preferred_element_type=jnp.float32) * SCALE
        local_top = jnp.max(logits, axis=1)
        label_term = jnp.sum(logits * onehot, axis=1)
        top = lax.pmax(local_top, "cls")
        total, picked = lax.psum(
            (jnp.sum(jnp.exp(logits - top[:, None]), axis=1), label_term), "cls"
        )
        lse = top + jnp.log(total)
        losses = lse - picked
        resid = (jnp.exp(logits - lse[:, None]) - onehot).astype(jnp.bfloat16)
        grad_local = (
            lax.dot_general(
                full_x, resid, (((0,), (0,)), ((), ())), preferred_element_type=jnp.float32
            )
            * SCALE
        )
        grad = lax.psum(grad_local, "img")
        master = shrink(master, grad, lam)
        operand = master.astype(jnp.bfloat16)
    rows = weights.shape[0]
    new_weights = lax.dynamic_slice_in_dim(master, lax.axis_index("img") * rows, rows, 0)
    return (new_weights, losses)


def solution(mesh):
    placed = (P(("grp", "img"), "cls"), P(("grp", "img")), P(("grp", "img"), "cls"), P("grp"))
    return jax.shard_map(
        fused if mesh.shape["cls"] == N else general,
        mesh=mesh,
        in_specs=placed,
        out_specs=(P(("grp", "img"), "cls"), P(("grp", "img"))),
        check_vma=False,
    )
```

```python
import functools
import math

import jax
import jax.numpy as jnp
from jax import lax
from jax.experimental import pallas as pl
from jax.experimental.pallas import tpu as pltpu
from jax.sharding import PartitionSpec as P

D = 1536
ITERS = 2
MESH = pl.DeviceIdType.MESH
SCALE = 1.0 / math.sqrt(D)

NX, NZ = 2, 4
N = NX * NZ
IMGS, WIDTH, CLS = 1024, 192, 128
HALF = WIDTH // 2
FEATS = D // 2
CHUNK = 256
CHUNKS = IMGS // CHUNK
BOTH = 2 * CHUNK
BLOCKS = D // 256
X_OWN, Z_OWN, X_MID, X_FAR, Z_FAR, Z_NEXT, UP_OWN, UP_FWD, UP_END, ACROSS = range(10)
SPLITS = (((0, 2), (2, 1), (3, 1)), ((0, 2), (2, 2)))
PEERS = (3, 7)
ORDER = (0, 1, 2, 3, 4, 5)


def shrink(master, grad, lam):
    moved = master - 16.0 * grad
    return jnp.sign(moved) * jnp.maximum(jnp.abs(moved) - lam, 0.0)


def kernel(x_hbm, lab_hbm, w_hbm, s_ref, out_ref, loss_ref,
           xd, labs, master, wb0, wb, ex0, ex, resid, rsend, gacc, hi, lo, ret,
           stat0, stat1, lall,
           load, e_send, e_recv, f_send, f_recv, w_send, w_recv, m_send, m_recv,
           q_send, q_recv, l_send, l_recv, r_send, r_recv):
    me = lax.axis_index("cls")
    img = lax.axis_index("img")
    grp = lax.axis_index("grp")
    z, x = me // NX, me % NX
    inner = jnp.logical_and(z > 0, z < NZ - 1)
    outer = jnp.logical_not(inner)
    zp = z + 1 - 2 * (z % 2)
    zo = NZ - 1 - z
    zf = NZ - 1 - zp

    def at_chip(sz, sx, core):
        return (grp, sz * NX + sx, core)

    mate = at_chip(z, x, 1 - img)
    side = at_chip(z, 1 - x, img)
    near = at_chip(zp, x, img)
    over = at_chip(zo, x, img)
    others = ((z, 1 - x), (zo, x), (zo, 1 - x))
    peers = [(sz, sx, img) for sz, sx in others]
    peers += [(sz, sx, 1 - img) for sz, sx in ((z, x),) + others]

    def rows(at, n):
        return pl.ds(pl.multiple_of(at, 16), n)

    def cols(k, half):
        return pl.ds(pl.multiple_of(k * BOTH + half * CHUNK, CHUNK), CHUNK)

    barrier = pltpu.get_barrier_semaphore()

    def greet(to):
        pl.semaphore_signal(barrier, inc=1, device_id=to, device_id_type=MESH)

    for core in range(2):
        greet(at_chip(zp, x, core))

    @pl.when(outer)
    def _():
        greet(side)

    @pl.when(inner)
    def _():
        for p in peers:
            greet(at_chip(*p))

    def remote(src, dst, sems, to):
        send, recv, at = sems
        return pltpu.make_async_remote_copy(
            src_ref=src, dst_ref=dst, send_sem=send.at[at], recv_sem=recv.at[at],
            device_id=to, device_id_type=MESH)

    def shard(sz, sx, at, n, k):
        return xd.at[rows((sz * NX + sx) * WIDTH + at, n), cols(k, img)]

    def piece(kind, k, sz, sx, at, n, to, own=False):
        place = shard(sz, sx, at, n, k)
        src = x_hbm.at[pl.ds(at, n), pl.ds(k * CHUNK, CHUNK)] if own else place
        return remote(src, place, (e_send, e_recv, (kind, k)), to)

    def change_piece(step, half, j):
        return pltpu.make_async_remote_copy(
            src_ref=ret.at[step, pl.ds(half * FEATS + 256 * j, 256)],
            dst_ref=ret.at[step, pl.ds(256 * j, 256)],
            send_sem=r_send.at[step, half * 3 + j], recv_sem=r_recv.at[step, j],
            device_id=at_chip(zp, x, half), device_id_type=MESH)

    def loss_piece():
        place = lall.at[img]
        return remote(place, place, (r_send, r_recv, (ITERS, 0)), near)

    label_load = pltpu.make_async_copy(lab_hbm, labs.at[img], load.at[6])

    def threshold():
        return 0.16 * jnp.exp2(s_ref[...].astype(jnp.float32))

    def step_to(old, change, lam):
        moved = old - change
        return moved - jnp.clip(moved, -lam, lam)

    def blocks(n, at=0):
        return [slice(at + 256 * j, at + 256 * j + 256) for j in range(n)]

    @pl.when(outer)
    def _():
        def own(k):
            return piece(UP_OWN, k, z, x, 0, WIDTH, near, own=True)

        def cross(part):
            at = (1 - part) * HALF
            places = [
                xd.at[rows((z * NX + sx) * WIDTH + at, HALF), pl.ds(0, IMGS)] for sx in (x, 1 - x)
            ]
            return [
                remote(src, dst, (e_send, e_recv, (ACROSS, part)), side)
                for src, dst in ((x_hbm.at[pl.ds(at, HALF)], places[0]), (places[1], places[1]))
            ]

        def onward(kind, k):
            at = (0, HALF)[kind == UP_FWD]
            r = rows((z * NX + 1 - x) * WIDTH + at, HALF)
            return remote(
                xd.at[r, pl.ds(k * CHUNK, CHUNK)], xd.at[r, cols(k, img)],
                (e_send, e_recv, (kind, k)), near)

        get = pltpu.make_async_copy(w_hbm, master.at[pl.ds(0, FEATS)], load.at[0])
        get.start()
        pl.semaphore_wait(barrier, 3)
        for k in range(CHUNKS):
            own(k).start()
        for part in range(2):
            cross(part)[0].start()
        get.wait()
        w = master[:FEATS]
        top = w.astype(jnp.bfloat16)
        hi[img] = top
        lo[img] = (w - top.astype(jnp.float32)).astype(jnp.bfloat16)

        def probe(buf, k):
            place = buf.at[img]
            return pltpu.make_async_remote_copy(
                src_ref=place, dst_ref=place, send_sem=w_send.at[k], recv_sem=w_recv.at[k, img],
                device_id=at_chip(zp, x, 1), device_id_type=MESH)

        probe(hi, 0).start()
        for part, kind in ((0, UP_FWD), (1, UP_END)):
            cross(part)[1].wait_recv()
            for k in range(CHUNKS):
                onward(kind, k).start()
        probe(lo, 1).start()
        lam = threshold()
        for j, r in enumerate(blocks(3)):
            change_piece(0, 0, j).wait_recv()
            master[r] = step_to(master[r], ret[0, r].astype(jnp.float32), lam)
        loss_piece().wait_recv()
        loss_ref[...] = lall[img]
        for j, r in enumerate(blocks(3)):
            change_piece(1, 0, j).wait_recv()
            out_ref[r] = step_to(master[r], ret[1, r].astype(jnp.float32), lam)
        for k in range(CHUNKS):
            own(k).wait_send()
            onward(UP_FWD, k).wait_send()
            onward(UP_END, k).wait_send()
        for part in range(2):
            cross(part)[0].wait_send()
        probe(hi, 0).wait_send()
        probe(lo, 1).wait_send()

    @pl.when(inner)
    def _():
        first, second = img == 0, img == 1

        def x_own(k, sx=x, own=True):
            return piece(X_OWN, k, z, sx, 0, WIDTH, side, own)

        def z_own(k, sz=z, own=True):
            return piece(Z_OWN, k, sz, x, 0, WIDTH, over, own)

        def x_mid(k, sx=x):
            return piece(X_MID, k, zo, sx, 0, WIDTH, side)

        def x_far(k, sx=x):
            return piece(X_FAR, k, zf, sx, 0, HALF, side)

        def z_far(k, sz=zp):
            return piece(Z_FAR, k, sz, x, 0, WIDTH, over)

        def z_next(k, sz=zp):
            return piece(Z_NEXT, k, sz, 1 - x, HALF, HALF, over)

        def share(k, sz, sx, at, n, own=False):
            place = shard(sz, sx, at, n, k)
            src = x_hbm.at[pl.ds(at, n), pl.ds(k * CHUNK, CHUNK)] if own else place
            remote(src, place, (f_send, f_recv, k), mate).start()

        def shared(k, half):
            place = xd.at[:, cols(k, half)]
            return remote(place, place, (f_send, f_recv, k), mate)

        def get_own(k):
            return pltpu.make_async_copy(
                x_hbm.at[:, pl.ds(k * CHUNK, CHUNK)], shard(z, x, 0, WIDTH, k), load.at[1 + k])

        def labels_to(half):
            return remote(labs.at[half], labs.at[half], (m_send, m_recv, 0), mate)

        upper = master.at[pl.ds(FEATS, FEATS)]

        def weights_to():
            return remote(w_hbm, upper, (m_send, m_recv, 1), mate)

        def out_to():
            return remote(upper, out_ref, (m_send, m_recv, 2), mate)

        def block_to(block):
            place = wb0.at[pl.ds(block * CLS, CLS)]
            return remote(place, place, (m_send, m_recv, 3), mate)

        def resid_to(k, half):
            return remote(
                rsend.at[:, pl.ds(k * CHUNK, CHUNK)], resid.at[:, cols(k, half)],
                (q_send, q_recv, k), mate)

        def probe_from(buf, k, half):
            place = buf.at[half]
            return pltpu.make_async_remote_copy(
                src_ref=place, dst_ref=place, send_sem=w_send.at[k], recv_sem=w_recv.at[k, half],
                device_id=at_chip(zp, x, half), device_id_type=MESH)

        get = pltpu.make_async_copy(w_hbm, master.at[pl.ds(0, FEATS)], load.at[0])

        @pl.when(first)
        def _():
            get.start()

        for k in range(CHUNKS):
            get_own(k).start()
        label_load.start()
        pl.semaphore_wait(barrier, 2 + PEERS[1])
        for k in range(CHUNKS):
            x_own(k).start()
            z_own(k).start()
        label_load.wait()
        labels_to(img).start()

        @pl.when(second)
        def _():
            weights_to().start()

        for k in range(CHUNKS):
            share(k, z, x, 0, WIDTH, own=True)

        @pl.when(first)
        def _():
            get.wait()
            weights_to().wait_recv()
            for r in blocks(BLOCKS):
                wb0[:CLS, r] = master[r].T.astype(jnp.bfloat16)

            block_to(0).start()

        for k in range(CHUNKS):
            z_own(k, zo, False).wait_recv()
            x_mid(k).start()
            share(k, zo, x, 0, WIDTH)
            piece(UP_OWN, k, zp, x, 0, WIDTH, near).wait_recv()
            z_far(k).start()
            share(k, zp, x, 0, WIDTH)
            x_own(k, 1 - x, False).wait_recv()
            share(k, z, 1 - x, 0, WIDTH)

        @pl.when(second)
        def _():
            for half in range(2):
                probe_from(hi, 0, half).wait_recv()
                for j, r in enumerate(blocks(3)):
                    part = hi[half, r].astype(jnp.float32)
                    q = blocks(3, half * FEATS)[j]
                    master[q] = part
                    wb0[CLS:, q] = part.T.astype(jnp.bfloat16)
            block_to(1).start()

        for k in range(CHUNKS):
            z_far(k, zf).wait_recv()
            x_far(k).start()
            share(k, zf, x, 0, WIDTH)
            piece(UP_FWD, k, zp, 1 - x, HALF, HALF, near).wait_recv()
            z_next(k).start()
            share(k, zp, 1 - x, HALF, HALF)
            get_own(k).wait()

        block_to(1 - img).wait_recv()

        def rank(sz, sx, core, step):
            chip = (sz - 1) * NX + sx
            return chip if step == 0 else chip * 2 + core

        mine = [rank(z, x, img, step) for step in range(ITERS)]
        stat = (stat0, stat1)
        firsts = [me * CLS, (zp * NX + x) * CLS]
        first_class = jnp.where(first, firsts[0], firsts[1])
        other_class = jnp.where(first, firsts[1], firsts[0])

        def stat_piece(step, p, i, where):
            at, n = SPLITS[step][p]
            width = (CHUNK, BOTH)[step]
            place = stat[step].at[where, :, pl.ds(at * width, n * width)]
            return remote(place, place, (l_send, l_recv, (step, p, i)), at_chip(*peers[i]))

        def send_stats(step, k):
            for p, (at, n) in enumerate(SPLITS[step]):
                if k == at + n - 1:
                    for i in range(PEERS[step]):
                        stat_piece(step, p, i, mine[step]).start()

        def wait_stats(step, p):
            for i, peer in enumerate(peers[:PEERS[step]]):
                stat_piece(step, p, i, rank(*peer, step)).wait_recv()

        def hot(half, k, base):
            cls = base + lax.broadcasted_iota(jnp.int32, (CLS, CHUNK), 0)
            return labs[half, :, k * CHUNK:k * CHUNK + CHUNK] == cls

        def hot_both(k):
            return jnp.concatenate([hot(half, k, first_class) for half in range(2)], axis=1)

        def span(k, n=1):
            return slice(k * BOTH, (k + n) * BOTH)

        def whole(buf, r, n):
            parts = [buf[m, 0:1, r] for m in range(n)]
            top = functools.reduce(jnp.maximum, parts)
            return top + jnp.log(sum(jnp.exp(v - top) for v in parts))

        def grad_slab(r, c):
            return lax.dot_general(
                xd[r, c], resid[:, c], (((1,), (1,)), ((), ())), preferred_element_type=jnp.float32)

        tops = []
        for k in range(CHUNKS):
            x_mid(k, 1 - x).wait_recv()
            piece(UP_END, k, zp, 1 - x, 0, HALF, near).wait_recv()
            x_far(k, 1 - x).wait_recv()
            z_next(k, zf).wait_recv()
            c = slice(k * CHUNK, k * CHUNK + CHUNK)
            logits = jnp.dot(wb0[...], xd[:, cols(k, img)], preferred_element_type=jnp.float32) * SCALE
            top = jnp.max(logits, axis=0, keepdims=True)
            e = jnp.exp(logits - top)
            ex0[0, :, c] = e[:CLS]
            ex0[1, :, c] = e[CLS:]
            stat0[mine[0], 0:1, c] = top + jnp.log(jnp.sum(e, axis=0, keepdims=True))
            tops.append(top)
            send_stats(0, k)
        for k in range(CHUNKS):
            share(k, zo, 1 - x, 0, WIDTH)
            share(k, zp, 1 - x, 0, HALF)
            share(k, zf, 1 - x, 0, HALF)
            share(k, zf, 1 - x, HALF, HALF)

        def residual(p):
            wait_stats(0, p)
            at, n = SPLITS[0][p]
            for k in range(at, at + n):
                c = slice(k * CHUNK, k * CHUNK + CHUNK)
                factor = jnp.exp(tops[k] - whole(stat0, c, PEERS[0] + 1))
                theirs = ex0[1 - img, :, c] * factor - jnp.where(hot(img, k, other_class), 1.0, 0.0)
                rsend[:, c] = theirs.astype(jnp.bfloat16)
                resid_to(k, img).start()
                ours = ex0[img, :, c] * factor - jnp.where(hot(img, k, first_class), 1.0, 0.0)
                resid[:, cols(k, img)] = ours.astype(jnp.bfloat16)

        def add_slab(k, half):
            for r in blocks(BLOCKS):
                gacc[r] += grad_slab(r, cols(k, half))

        def their_chunk(k):
            resid_to(k, 1 - img).wait_recv()
            shared(k, 1 - img).wait_recv()

        lam = threshold()
        gacc[...] = jnp.zeros_like(gacc)
        groups = [range(at, at + n) for at, n in SPLITS[0]]
        for p, ks in enumerate(groups):
            residual(p)
            for k in (groups[p - 1] if p > 0 else ()):
                their_chunk(k)
                add_slab(k, 1 - img)
            for k in ks:
                add_slab(k, img)

        @pl.when(second)
        def _():
            for half in range(2):
                probe_from(lo, 1, half).wait_recv()
                q = slice(half * FEATS, half * FEATS + FEATS)
                master[q] += lo[half].astype(jnp.float32)

        their_chunk(CHUNKS - 1)
        for r in blocks(BLOCKS):
            change = (gacc[r] + grad_slab(r, cols(CHUNKS - 1, 1 - img))) * (16.0 * SCALE)
            new = step_to(master[r], change, lam)
            master[r] = new
            wb[:, r] = new.T.astype(jnp.bfloat16)
            ret[0, r] = change.astype(jnp.bfloat16)

        @pl.when(second)
        def _():
            for j in range(BLOCKS):
                change_piece(0, j // 3, j % 3).start()

        labels_to(1 - img).wait_recv()
        tops = []
        for k in range(CHUNKS):
            r = span(k)
            logits = jnp.dot(wb[...], xd[:, r], preferred_element_type=jnp.float32) * SCALE
            top = jnp.max(logits, axis=0, keepdims=True)
            e = jnp.exp(logits - top)
            ex[:, r] = e
            stat1[mine[1], 0:1, r] = top + jnp.log(jnp.sum(e, axis=0, keepdims=True))
            stat1[mine[1], 1:2, r] = jnp.sum(jnp.where(hot_both(k), logits, 0.0), axis=0, keepdims=True)
            tops.append(top)
            send_stats(1, k)
        ends = len(SPLITS[1]) - 1
        for p, (at, n) in enumerate(SPLITS[1]):
            wait_stats(1, p)
            for k in range(at, at + n):
                r = span(k)
                lse = whole(stat1, r, PEERS[1] + 1)
                loss = lse - sum(stat1[m, 1:2, r] for m in range(PEERS[1] + 1))
                for i in range(0, BOTH, 128):
                    half, row = i // CHUNK, (k * CHUNK + i % CHUNK) // 128
                    lall[half, row:row + 1, :] = loss[:, i:i + 128]
                prob = ex[:, r] * jnp.exp(tops[k] - lse)
                resid[:, r] = (prob - jnp.where(hot_both(k), 1.0, 0.0)).astype(jnp.bfloat16)
            if p < ends:
                for r in blocks(BLOCKS):
                    part = grad_slab(r, span(at, n))
                    gacc[r] = part if p == 0 else gacc[r] + part
        loss_piece().start()
        for j in ORDER:
            r = blocks(BLOCKS)[j]
            change = (gacc[r] + grad_slab(r, span(*SPLITS[1][ends]))) * (16.0 * SCALE)
            ret[1, r] = change.astype(jnp.bfloat16)

            @pl.when(second)
            def _(j=j):
                change_piece(1, j // 3, j % 3).start()

            new = step_to(master[r], change, lam)
            if j < 3:
                @pl.when(first)
                def _(r=r, new=new):
                    out_ref[r] = new
            else:
                master[r] = new
        loss_ref[...] = lall[img]

        @pl.when(first)
        def _():
            out_to().start()

        @pl.when(second)
        def _():
            out_to().wait_recv()

        for k in range(CHUNKS):
            for c in (x_own(k), z_own(k), x_mid(k), x_far(k), z_far(k), z_next(k)):
                c.wait_send()
            shared(k, img).wait_send()
            resid_to(k, img).wait_send()
        labels_to(img).wait_send()
        block_to(img).wait_send()

        @pl.when(first)
        def _():
            out_to().wait_send()

        @pl.when(second)
        def _():
            weights_to().wait_send()
            for step in range(ITERS):
                for j in range(BLOCKS):
                    change_piece(step, j // 3, j % 3).wait_send()

        for step in range(ITERS):
            for p in range(len(SPLITS[step])):
                for i in range(PEERS[step]):
                    stat_piece(step, p, i, mine[step]).wait_send()
        loss_piece().wait_send()


def fused(embeddings, labels, weights, strength):
    vmem = pl.BlockSpec(memory_space=pltpu.VMEM)
    hbm = pl.BlockSpec(memory_space=pl.ANY)
    f32, bf16 = jnp.float32, jnp.bfloat16
    dma = pltpu.SemaphoreType.DMA
    groups = max(len(v) for v in SPLITS)

    def pinned(array):
        return pltpu.with_memory_space_constraint(array, pltpu.HBM)

    new_weights, losses = pl.pallas_call(
        kernel,
        out_shape=(
            jax.ShapeDtypeStruct((FEATS, CLS), f32),
            jax.ShapeDtypeStruct((IMGS // 128, 128), f32),
        ),
        in_specs=[hbm, hbm, hbm, vmem],
        out_specs=(vmem, vmem),
        scratch_shapes=[
            pltpu.VMEM((D, 2 * IMGS), bf16),
            pltpu.VMEM((2, 1, IMGS), jnp.int32),
            pltpu.VMEM((D, CLS), f32),
            pltpu.VMEM((2 * CLS, D), bf16),
            pltpu.VMEM((CLS, D), bf16),
            pltpu.VMEM((2, CLS, IMGS), f32),
            pltpu.VMEM((CLS, 2 * IMGS), f32),
            pltpu.VMEM((CLS, 2 * IMGS), bf16),
            pltpu.VMEM((CLS, IMGS), bf16),
            pltpu.VMEM((D, CLS), f32),
            pltpu.VMEM((2, FEATS, CLS), bf16),
            pltpu.VMEM((2, FEATS, CLS), bf16),
            pltpu.VMEM((ITERS, D, CLS), bf16),
            pltpu.VMEM((PEERS[0] + 1, 1, IMGS), f32),
            pltpu.VMEM((PEERS[1] + 1, 2, 2 * IMGS), f32),
            pltpu.VMEM((2, IMGS // 128, 128), f32),
            dma((3 + CHUNKS,)),
            dma((10, CHUNKS)),
            dma((10, CHUNKS)),
            dma((CHUNKS,)),
            dma((CHUNKS,)),
            dma((2,)),
            dma((2, 2)),
            dma((4,)),
            dma((4,)),
            dma((CHUNKS,)),
            dma((CHUNKS,)),
            dma((ITERS, groups, PEERS[1])),
            dma((ITERS, groups, PEERS[1])),
            dma((ITERS + 1, BLOCKS)),
            dma((ITERS + 1, BLOCKS)),
        ],
        compiler_params=pltpu.CompilerParams(
            collective_id=0, has_side_effects=True, vmem_limit_bytes=32 * 1024 * 1024
        ),
    )(
        pinned(embeddings.T), pinned(labels.reshape(1, IMGS)), pinned(weights),
        strength.reshape(1, 1),
    )
    return new_weights, losses.reshape(IMGS)


def general(embeddings, labels, weights, strength):
    lam = 16.0 * 0.01 * jnp.exp2(strength[0].astype(jnp.float32))
    full_x = lax.all_gather(embeddings, "cls", axis=1, tiled=True)
    cls_width = weights.shape[1]
    first_class = lax.axis_index("cls") * cls_width
    classes = first_class + lax.iota(jnp.int32, cls_width)
    onehot = (labels[:, None] == classes[None, :]).astype(jnp.float32)
    master = lax.all_gather(weights, "img", axis=0, tiled=True)
    operand = master.astype(jnp.bfloat16)
    losses = jnp.zeros((labels.shape[0],), jnp.float32)
    for step in range(ITERS):
        logits = jnp.dot(full_x, operand, preferred_element_type=jnp.float32) * SCALE
        local_top = jnp.max(logits, axis=1)
        label_term = jnp.sum(logits * onehot, axis=1)
        top = lax.pmax(local_top, "cls")
        total, picked = lax.psum(
            (jnp.sum(jnp.exp(logits - top[:, None]), axis=1), label_term), "cls"
        )
        lse = top + jnp.log(total)
        losses = lse - picked
        resid = (jnp.exp(logits - lse[:, None]) - onehot).astype(jnp.bfloat16)
        grad_local = (
            lax.dot_general(
                full_x, resid, (((0,), (0,)), ((), ())), preferred_element_type=jnp.float32
            )
            * SCALE
        )
        grad = lax.psum(grad_local, "img")
        master = shrink(master, grad, lam)
        operand = master.astype(jnp.bfloat16)
    rows = weights.shape[0]
    new_weights = lax.dynamic_slice_in_dim(master, lax.axis_index("img") * rows, rows, 0)
    return (new_weights, losses)


def solution(mesh):
    placed = (P(("grp", "img"), "cls"), P(("grp", "img")), P(("grp", "img"), "cls"), P("grp"))
    return jax.shard_map(
        fused if mesh.shape["cls"] == N else general,
        mesh=mesh,
        in_specs=placed,
        out_specs=(P(("grp", "img"), "cls"), P(("grp", "img"))),
        check_vma=False,
    )
```

```python
import functools
import math

import jax
import jax.numpy as jnp
from jax import lax
from jax.experimental import pallas as pl
from jax.experimental.pallas import tpu as pltpu
from jax.sharding import PartitionSpec as P

D = 1536
ITERS = 2
MESH = pl.DeviceIdType.MESH
SCALE = 1.0 / math.sqrt(D)

NX, NZ = 2, 4
N = NX * NZ
IMGS, WIDTH, CLS = 1024, 192, 128
HALF = WIDTH // 2
FEATS = D // 2
CHUNK = 256
CHUNKS = IMGS // CHUNK
BOTH = 2 * CHUNK
BLOCKS = D // 256
X_OWN, Z_OWN, X_MID, X_FAR, Z_FAR, Z_NEXT, UP_OWN, UP_FWD, UP_END, ACROSS = range(10)
SPLITS = (((0, 2), (2, 1), (3, 1)), ((0, 2), (2, 2)))
PEERS = 7


def shrink(master, grad, lam):
    moved = master - 16.0 * grad
    return jnp.sign(moved) * jnp.maximum(jnp.abs(moved) - lam, 0.0)


def kernel(x_hbm, lab_hbm, w_hbm, s_ref, out_ref, loss_ref,
           xd, labs, master, wb0, wb, logit, other, ex, resid, gacc, hi, lo, ret,
           stat0, stat1, lall,
           load, e_send, e_recv, f_send, f_recv, w_send, w_recv, m_send, m_recv,
           q_send, q_recv, l_send, l_recv, r_send, r_recv):
    me = lax.axis_index("cls")
    img = lax.axis_index("img")
    grp = lax.axis_index("grp")
    z, x = me // NX, me % NX
    inner = jnp.logical_and(z > 0, z < NZ - 1)
    outer = jnp.logical_not(inner)
    zp = z + 1 - 2 * (z % 2)
    zo = NZ - 1 - z
    zf = NZ - 1 - zp

    def at_chip(sz, sx, core):
        return (grp, sz * NX + sx, core)

    mate = at_chip(z, x, 1 - img)
    side = at_chip(z, 1 - x, img)
    near = at_chip(zp, x, img)
    over = at_chip(zo, x, img)
    others = ((z, 1 - x), (zo, x), (zo, 1 - x))
    peers = [(sz, sx, core) for sz, sx in others for core in (img, 1 - img)] + [(z, x, 1 - img)]

    def rows(at, n):
        return pl.ds(pl.multiple_of(at, 16), n)

    def cols(k, half):
        return pl.ds(pl.multiple_of(k * BOTH + half * CHUNK, CHUNK), CHUNK)

    barrier = pltpu.get_barrier_semaphore()

    def greet(to):
        pl.semaphore_signal(barrier, inc=1, device_id=to, device_id_type=MESH)

    for core in range(2):
        greet(at_chip(zp, x, core))

    @pl.when(outer)
    def _():
        greet(side)

    @pl.when(inner)
    def _():
        for p in peers:
            greet(at_chip(*p))

    def remote(src, dst, sems, to):
        send, recv, at = sems
        return pltpu.make_async_remote_copy(
            src_ref=src, dst_ref=dst, send_sem=send.at[at], recv_sem=recv.at[at],
            device_id=to, device_id_type=MESH)

    def shard(sz, sx, at, n, k):
        return xd.at[rows((sz * NX + sx) * WIDTH + at, n), cols(k, img)]

    def piece(kind, k, sz, sx, at, n, to, own=False):
        place = shard(sz, sx, at, n, k)
        src = x_hbm.at[pl.ds(at, n), pl.ds(k * CHUNK, CHUNK)] if own else place
        return remote(src, place, (e_send, e_recv, (kind, k)), to)

    def change_piece(step, half, j):
        return pltpu.make_async_remote_copy(
            src_ref=ret.at[step, pl.ds(half * FEATS + 256 * j, 256)],
            dst_ref=ret.at[step, pl.ds(256 * j, 256)],
            send_sem=r_send.at[step, half * 3 + j], recv_sem=r_recv.at[step, j],
            device_id=at_chip(zp, x, half), device_id_type=MESH)

    def loss_piece(half):
        place = lall.at[half]
        return pltpu.make_async_remote_copy(
            src_ref=place, dst_ref=place, send_sem=r_send.at[ITERS, half],
            recv_sem=r_recv.at[ITERS, 0], device_id=at_chip(zp, x, half), device_id_type=MESH)

    label_load = pltpu.make_async_copy(lab_hbm, labs.at[img], load.at[6])

    def threshold():
        return 0.16 * jnp.exp2(jnp.full((1, 1), s_ref[0], jnp.int32).astype(jnp.float32))

    def step_to(old, change, lam):
        moved = old - change
        return moved - jnp.clip(moved, -lam, lam)

    def blocks(n, at=0):
        return [slice(at + 256 * j, at + 256 * j + 256) for j in range(n)]

    @pl.when(outer)
    def _():
        def own(k):
            return piece(UP_OWN, k, z, x, 0, WIDTH, near, own=True)

        def cross(part):
            at = (1 - part) * HALF
            places = [
                xd.at[rows((z * NX + sx) * WIDTH + at, HALF), pl.ds(0, IMGS)] for sx in (x, 1 - x)
            ]
            return [
                remote(src, dst, (e_send, e_recv, (ACROSS, part)), side)
                for src, dst in ((x_hbm.at[pl.ds(at, HALF)], places[0]), (places[1], places[1]))
            ]

        def onward(kind, k):
            at = (0, HALF)[kind == UP_FWD]
            r = rows((z * NX + 1 - x) * WIDTH + at, HALF)
            return remote(
                xd.at[r, pl.ds(k * CHUNK, CHUNK)], xd.at[r, cols(k, img)],
                (e_send, e_recv, (kind, k)), near)

        get = pltpu.make_async_copy(w_hbm, master.at[pl.ds(0, FEATS)], load.at[0])
        get.start()
        pl.semaphore_wait(barrier, 3)
        for k in range(CHUNKS):
            own(k).start()
        for part in range(2):
            cross(part)[0].start()
        get.wait()
        w = master[:FEATS]
        top = w.astype(jnp.bfloat16)
        hi[img] = top
        lo[img] = (w - top.astype(jnp.float32)).astype(jnp.bfloat16)

        def probe(buf, k, at, n):
            place = buf.at[img, pl.ds(at, n)]
            return pltpu.make_async_remote_copy(
                src_ref=place, dst_ref=place, send_sem=w_send.at[k], recv_sem=w_recv.at[k, img],
                device_id=at_chip(zp, x, 1), device_id_type=MESH)

        probes = [probe(hi, 0, 0, FEATS)] + [probe(lo, 1 + j, 256 * j, 256) for j in range(3)]
        probes[0].start()
        for part, kind in ((0, UP_FWD), (1, UP_END)):
            cross(part)[1].wait_recv()
            for k in range(CHUNKS):
                onward(kind, k).start()
        for c in probes[1:]:
            c.start()
        lam = threshold()
        for j, r in enumerate(blocks(3)):
            change_piece(0, 0, j).wait_recv()
            master[r] = step_to(master[r], ret[0, r].astype(jnp.float32), lam)
        loss_piece(img).wait_recv()
        loss_ref[...] = lall[img]
        for j, r in enumerate(blocks(3)):
            change_piece(1, 0, j).wait_recv()
            out_ref[r] = step_to(master[r], ret[1, r].astype(jnp.float32), lam)
        for k in range(CHUNKS):
            own(k).wait_send()
            onward(UP_FWD, k).wait_send()
            onward(UP_END, k).wait_send()
        for part in range(2):
            cross(part)[0].wait_send()
        for c in probes:
            c.wait_send()

    @pl.when(inner)
    def _():
        first, second = img == 0, img == 1

        def x_own(k, sx=x, own=True):
            return piece(X_OWN, k, z, sx, 0, WIDTH, side, own)

        def z_own(k, sz=z, own=True):
            return piece(Z_OWN, k, sz, x, 0, WIDTH, over, own)

        def x_mid(k, sx=x):
            return piece(X_MID, k, zo, sx, 0, WIDTH, side)

        def x_far(k, sx=x):
            return piece(X_FAR, k, zf, sx, 0, HALF, side)

        def z_far(k, sz=zp):
            return piece(Z_FAR, k, sz, x, 0, WIDTH, over)

        def z_next(k, sz=zp):
            return piece(Z_NEXT, k, sz, 1 - x, HALF, HALF, over)

        def share(k, sz, sx, at, n, own=False):
            place = shard(sz, sx, at, n, k)
            src = x_hbm.at[pl.ds(at, n), pl.ds(k * CHUNK, CHUNK)] if own else place
            remote(src, place, (f_send, f_recv, k), mate).start()

        def shared(k, half):
            place = xd.at[:, cols(k, half)]
            return remote(place, place, (f_send, f_recv, k), mate)

        def get_own(k):
            return pltpu.make_async_copy(
                x_hbm.at[:, pl.ds(k * CHUNK, CHUNK)], shard(z, x, 0, WIDTH, k), load.at[1 + k])

        def labels_to(half):
            return remote(labs.at[half], labs.at[half], (m_send, m_recv, 0), mate)

        upper = master.at[pl.ds(FEATS, FEATS)]

        def weights_to():
            return remote(w_hbm, upper, (m_send, m_recv, 1), mate)

        def out_to():
            return remote(upper, out_ref, (m_send, m_recv, 2), mate)

        def block_to(block):
            place = wb0.at[pl.ds(block * CLS, CLS)]
            return remote(place, place, (m_send, m_recv, 3), mate)

        def logit_to(k):
            c = pl.ds(k * CHUNK, CHUNK)
            return remote(logit.at[1 - img, :, c], other.at[:, c], (q_send, q_recv, k), mate)

        def probe_from(buf, k, half, at, n):
            place = buf.at[half, pl.ds(at, n)]
            return pltpu.make_async_remote_copy(
                src_ref=place, dst_ref=place, send_sem=w_send.at[k], recv_sem=w_recv.at[k, half],
                device_id=at_chip(zp, x, half), device_id_type=MESH)

        get = pltpu.make_async_copy(w_hbm, master.at[pl.ds(0, FEATS)], load.at[0])

        @pl.when(first)
        def _():
            get.start()

        for k in range(CHUNKS):
            get_own(k).start()
        label_load.start()
        pl.semaphore_wait(barrier, 2 + PEERS)
        for k in range(CHUNKS):
            x_own(k).start()
            z_own(k).start()
        label_load.wait()
        labels_to(img).start()

        @pl.when(second)
        def _():
            weights_to().start()

        for k in range(CHUNKS):
            share(k, z, x, 0, WIDTH, own=True)

        @pl.when(first)
        def _():
            get.wait()
            weights_to().wait_recv()
            for r in blocks(BLOCKS):
                wb0[:CLS, r] = master[r].T.astype(jnp.bfloat16)

            block_to(0).start()

        for k in range(CHUNKS):
            z_own(k, zo, False).wait_recv()
            x_mid(k).start()
            share(k, zo, x, 0, WIDTH)
            piece(UP_OWN, k, zp, x, 0, WIDTH, near).wait_recv()
            z_far(k).start()
            share(k, zp, x, 0, WIDTH)
            x_own(k, 1 - x, False).wait_recv()
            share(k, z, 1 - x, 0, WIDTH)

        @pl.when(second)
        def _():
            for half in range(2):
                probe_from(hi, 0, half, 0, FEATS).wait_recv()
                for j, r in enumerate(blocks(3)):
                    part = hi[half, r].astype(jnp.float32)
                    q = blocks(3, half * FEATS)[j]
                    master[q] = part
                    wb0[CLS:, q] = part.T.astype(jnp.bfloat16)
            block_to(1).start()

        for k in range(CHUNKS):
            z_far(k, zf).wait_recv()
            x_far(k).start()
            share(k, zf, x, 0, WIDTH)
            piece(UP_FWD, k, zp, 1 - x, HALF, HALF, near).wait_recv()
            z_next(k).start()
            share(k, zp, 1 - x, HALF, HALF)
            get_own(k).wait()

        block_to(1 - img).wait_recv()

        def rank(sz, sx, core):
            return ((sz - 1) * NX + sx) * 2 + core

        mine = rank(z, x, img)
        stat = (stat0, stat1)
        first_class = jnp.where(first, me, zp * NX + x) * CLS

        def stat_piece(step, p, i, where):
            at, n = SPLITS[step][p]
            width = (CHUNK, BOTH)[step]
            place = stat[step].at[where, :, pl.ds(at * width, n * width)]
            return remote(place, place, (l_send, l_recv, (step, p, i)), at_chip(*peers[i]))

        def send_stats(step, k):
            for p, (at, n) in enumerate(SPLITS[step]):
                if k == at + n - 1:
                    for i in range(PEERS):
                        stat_piece(step, p, i, mine).start()

        def wait_stats(step, p):
            for i, peer in enumerate(peers):
                stat_piece(step, p, i, rank(*peer)).wait_recv()

        def hot(half, k):
            cls = first_class + lax.broadcasted_iota(jnp.int32, (CLS, CHUNK), 0)
            return labs[half, :, k * CHUNK:k * CHUNK + CHUNK] == cls

        def hot_both(k):
            return jnp.concatenate([hot(half, k) for half in range(2)], axis=1)

        def span(k, n=1):
            return slice(k * BOTH, (k + n) * BOTH)

        def whole(parts):
            top = functools.reduce(jnp.maximum, parts)
            return top + jnp.log(sum(jnp.exp(v - top) for v in parts))

        def grad_slab(r, c):
            return lax.dot_general(
                xd[r, c], resid[:, c], (((1,), (1,)), ((), ())), preferred_element_type=jnp.float32)

        for k in range(CHUNKS):
            x_mid(k, 1 - x).wait_recv()
            piece(UP_END, k, zp, 1 - x, 0, HALF, near).wait_recv()
            x_far(k, 1 - x).wait_recv()
            z_next(k, zf).wait_recv()
            c = slice(k * CHUNK, k * CHUNK + CHUNK)
            logits = jnp.dot(wb0[...], xd[:, cols(k, img)], preferred_element_type=jnp.float32) * SCALE
            top = jnp.max(logits, axis=0, keepdims=True)
            total = jnp.sum(jnp.exp(logits - top), axis=0, keepdims=True)
            stat0[mine, 0:1, c] = top + jnp.log(total)
            send_stats(0, k)
            logit[0, :, c] = logits[:CLS]
            logit[1, :, c] = logits[CLS:]
            logit_to(k).start()
            share(k, zo, 1 - x, 0, WIDTH)
            share(k, zp, 1 - x, 0, HALF)
            share(k, zf, 1 - x, 0, HALF)
            share(k, zf, 1 - x, HALF, HALF)

        def residual(p):
            wait_stats(0, p)
            at, n = SPLITS[0][p]
            for k in range(at, at + n):
                c = slice(k * CHUNK, k * CHUNK + CHUNK)
                logit_to(k).wait_recv()
                for half, values in ((img, logit[img, :, c]), (1 - img, other[:, c])):
                    lse = whole([stat0[2 * chip + half, 0:1, c] for chip in range(4)])
                    wrong = jnp.exp(values - lse) - jnp.where(hot(half, k), 1.0, 0.0)
                    resid[:, cols(k, half)] = wrong.astype(jnp.bfloat16)

        lam = threshold()
        labels_to(1 - img).wait_recv()
        ends = len(SPLITS[0]) - 1
        for p, (at, n) in enumerate(SPLITS[0]):
            residual(p)
            for k in range(at, at + n):
                shared(k, 1 - img).wait_recv()
            if p < ends:
                for r in blocks(BLOCKS):
                    part = grad_slab(r, span(at, n))
                    gacc[r] = part if p == 0 else gacc[r] + part
        @pl.when(second)
        def _():
            for j in range(BLOCKS):
                probe_from(lo, 1 + j % 3, j // 3, 256 * (j % 3), 256).wait_recv()
            for half in range(2):
                q = slice(half * FEATS, half * FEATS + FEATS)
                master[q] += lo[half].astype(jnp.float32)

        for r in blocks(BLOCKS):

            change = (gacc[r] + grad_slab(r, span(*SPLITS[0][ends]))) * (16.0 * SCALE)
            new = step_to(master[r], change, lam)
            master[r] = new
            wb[:, r] = new.T.astype(jnp.bfloat16)
            ret[0, r] = change.astype(jnp.bfloat16)

        @pl.when(second)
        def _():
            for j in range(BLOCKS):
                change_piece(0, j // 3, j % 3).start()

        tops = []
        for k in range(CHUNKS):
            r = span(k)
            logits = jnp.dot(wb[...], xd[:, r], preferred_element_type=jnp.float32) * SCALE
            top = jnp.max(logits, axis=0, keepdims=True)
            e = jnp.exp(logits - top)
            ex[:, r] = e
            stat1[mine, 0:1, r] = top + jnp.log(jnp.sum(e, axis=0, keepdims=True))
            stat1[mine, 1:2, r] = jnp.sum(jnp.where(hot_both(k), logits, 0.0), axis=0, keepdims=True)
            tops.append(top)
            send_stats(1, k)
        ends = len(SPLITS[1]) - 1
        for p, (at, n) in enumerate(SPLITS[1]):
            wait_stats(1, p)
            for k in range(at, at + n):
                r = span(k)
                lse = whole([stat1[m, 0:1, r] for m in range(PEERS + 1)])
                loss = lse - sum(stat1[m, 1:2, r] for m in range(PEERS + 1))
                for i in range(0, BOTH, 128):
                    half, row = i // CHUNK, (k * CHUNK + i % CHUNK) // 128
                    lall[half, row:row + 1, :] = loss[:, i:i + 128]
                prob = ex[:, r] * jnp.exp(tops[k] - lse)
                resid[:, r] = (prob - jnp.where(hot_both(k), 1.0, 0.0)).astype(jnp.bfloat16)
            if p < ends:
                for r in blocks(BLOCKS):
                    part = grad_slab(r, span(at, n))
                    gacc[r] = part if p == 0 else gacc[r] + part
        def last_change(r):
            return (gacc[r] + grad_slab(r, span(*SPLITS[1][ends]))) * (16.0 * SCALE)

        @pl.when(second)
        def _():
            for j, r in enumerate(blocks(BLOCKS)):
                ret[1, r] = last_change(r).astype(jnp.bfloat16)
                change_piece(1, j // 3, j % 3).start()

        @pl.when(first)
        def _():
            for half in range(2):
                loss_piece(half).start()
            for j, r in enumerate(blocks(BLOCKS)):
                new = step_to(master[r], last_change(r), lam)
                if j < 3:
                    out_ref[r] = new
                else:
                    master[r] = new

        loss_ref[...] = lall[img]

        @pl.when(first)
        def _():
            out_to().start()

        @pl.when(second)
        def _():
            out_to().wait_recv()

        for k in range(CHUNKS):
            for c in (x_own(k), z_own(k), x_mid(k), x_far(k), z_far(k), z_next(k)):
                c.wait_send()
            shared(k, img).wait_send()
            logit_to(k).wait_send()
        labels_to(img).wait_send()
        block_to(img).wait_send()

        @pl.when(first)
        def _():
            out_to().wait_send()
            for half in range(2):
                loss_piece(half).wait_send()

        @pl.when(second)
        def _():
            weights_to().wait_send()
            for step in range(ITERS):
                for j in range(BLOCKS):
                    change_piece(step, j // 3, j % 3).wait_send()

        for step in range(ITERS):
            for p in range(len(SPLITS[step])):
                for i in range(PEERS):
                    stat_piece(step, p, i, mine).wait_send()


def store(weights_ref, losses_ref, weights_out, losses_out, flat, sems):
    copies = [
        pltpu.make_async_copy(weights_ref, weights_out, sems.at[0]),
        pltpu.make_async_copy(flat, losses_out, sems.at[1]),
    ]
    copies[0].start()
    for i in range(IMGS // 128):
        flat[pl.ds(128 * i, 128)] = losses_ref[i]
    copies[1].start()
    for c in copies:
        c.wait()


def fused(embeddings, labels, weights, strength):
    vmem = pl.BlockSpec(memory_space=pltpu.VMEM)
    hbm = pl.BlockSpec(memory_space=pl.ANY)
    f32, bf16 = jnp.float32, jnp.bfloat16
    dma = pltpu.SemaphoreType.DMA
    groups = max(len(v) for v in SPLITS)

    def pinned(array):
        return pltpu.with_memory_space_constraint(array, pltpu.HBM)

    new_weights, losses = pl.pallas_call(
        kernel,
        out_shape=(
            pltpu.VMEM((FEATS, CLS), f32),
            pltpu.VMEM((IMGS // 128, 128), f32),
        ),
        in_specs=[hbm, hbm, hbm, pl.BlockSpec(memory_space=pltpu.SMEM)],
        out_specs=(vmem, vmem),
        scratch_shapes=[
            pltpu.VMEM((D, 2 * IMGS), bf16),
            pltpu.VMEM((2, 1, IMGS), jnp.int32),
            pltpu.VMEM((D, CLS), f32),
            pltpu.VMEM((2 * CLS, D), bf16),
            pltpu.VMEM((CLS, D), bf16),
            pltpu.VMEM((2, CLS, IMGS), f32),
            pltpu.VMEM((CLS, IMGS), f32),
            pltpu.VMEM((CLS, 2 * IMGS), f32),
            pltpu.VMEM((CLS, 2 * IMGS), bf16),
            pltpu.VMEM((D, CLS), f32),
            pltpu.VMEM((2, FEATS, CLS), bf16),
            pltpu.VMEM((2, FEATS, CLS), bf16),
            pltpu.VMEM((ITERS, D, CLS), bf16),
            pltpu.VMEM((PEERS + 1, 1, IMGS), f32),
            pltpu.VMEM((PEERS + 1, 2, 2 * IMGS), f32),
            pltpu.VMEM((2, IMGS // 128, 128), f32),
            dma((3 + CHUNKS,)),
            dma((10, CHUNKS)),
            dma((10, CHUNKS)),
            dma((CHUNKS,)),
            dma((CHUNKS,)),
            dma((4,)),
            dma((4, 2)),
            dma((4,)),
            dma((4,)),
            dma((CHUNKS,)),
            dma((CHUNKS,)),
            dma((ITERS, groups, PEERS)),
            dma((ITERS, groups, PEERS)),
            dma((ITERS + 1, BLOCKS)),
            dma((ITERS + 1, BLOCKS)),
        ],
        compiler_params=pltpu.CompilerParams(
            collective_id=0, has_side_effects=True, vmem_limit_bytes=32 * 1024 * 1024
        ),
    )(
        pinned(embeddings.T), pinned(labels.reshape(1, IMGS)), pinned(weights),
        strength,
    )

    def kept(array):
        return pltpu.with_memory_space_constraint(array, pltpu.VMEM)

    return pl.pallas_call(
        store,
        out_shape=(
            jax.ShapeDtypeStruct((FEATS, CLS), f32),
            jax.ShapeDtypeStruct((IMGS,), f32),
        ),
        in_specs=[vmem, vmem],
        out_specs=(hbm, hbm),
        scratch_shapes=[pltpu.VMEM((IMGS,), f32), dma((2,))],
    )(kept(new_weights), kept(losses))


def general(embeddings, labels, weights, strength):
    lam = 16.0 * 0.01 * jnp.exp2(strength[0].astype(jnp.float32))
    full_x = lax.all_gather(embeddings, "cls", axis=1, tiled=True)
    cls_width = weights.shape[1]
    first_class = lax.axis_index("cls") * cls_width
    classes = first_class + lax.iota(jnp.int32, cls_width)
    onehot = (labels[:, None] == classes[None, :]).astype(jnp.float32)
    master = lax.all_gather(weights, "img", axis=0, tiled=True)
    operand = master.astype(jnp.bfloat16)
    losses = jnp.zeros((labels.shape[0],), jnp.float32)
    for step in range(ITERS):
        logits = jnp.dot(full_x, operand, preferred_element_type=jnp.float32) * SCALE
        local_top = jnp.max(logits, axis=1)
        label_term = jnp.sum(logits * onehot, axis=1)
        top = lax.pmax(local_top, "cls")
        total, picked = lax.psum(
            (jnp.sum(jnp.exp(logits - top[:, None]), axis=1), label_term), "cls"
        )
        lse = top + jnp.log(total)
        losses = lse - picked
        resid = (jnp.exp(logits - lse[:, None]) - onehot).astype(jnp.bfloat16)
        grad_local = (
            lax.dot_general(
                full_x, resid, (((0,), (0,)), ((), ())), preferred_element_type=jnp.float32
            )
            * SCALE
        )
        grad = lax.psum(grad_local, "img")
        master = shrink(master, grad, lam)
        operand = master.astype(jnp.bfloat16)
    rows = weights.shape[0]
    new_weights = lax.dynamic_slice_in_dim(master, lax.axis_index("img") * rows, rows, 0)
    return (new_weights, losses)


def solution(mesh):
    placed = (P(("grp", "img"), "cls"), P(("grp", "img")), P(("grp", "img"), "cls"), P("grp"))
    return jax.shard_map(
        fused if mesh.shape["cls"] == N else general,
        mesh=mesh,
        in_specs=placed,
        out_specs=(P(("grp", "img"), "cls"), P(("grp", "img"))),
        check_vma=False,
    )
```

```python
import functools
import math

import jax
import jax.numpy as jnp
from jax import lax
from jax.experimental import pallas as pl
from jax.experimental.pallas import tpu as pltpu
from jax.sharding import PartitionSpec as P

D = 1536
ITERS = 2
MESH = pl.DeviceIdType.MESH
SCALE = 1.0 / math.sqrt(D)

NX, NZ = 2, 4
N = NX * NZ
IMGS, WIDTH, CLS = 1024, 192, 128
HALF = WIDTH // 2
FEATS = D // 2
CHUNK = 256
CHUNKS = IMGS // CHUNK
BOTH = 2 * CHUNK
BLOCKS = D // 256
X_OWN, Z_OWN, X_MID, X_FAR, Z_FAR, Z_NEXT, UP_OWN, UP_FWD, UP_END, ACROSS = range(10)
SPLITS = (((0, 2), (2, 1), (3, 1)), ((0, 2), (2, 2)))
PEERS = 7


def shrink(master, grad, lam):
    moved = master - 16.0 * grad
    return jnp.sign(moved) * jnp.maximum(jnp.abs(moved) - lam, 0.0)


def kernel(x_hbm, lab_hbm, w_hbm, s_ref, out_ref, loss_ref,
           xd, labs, master, wb0, wb, logit, other, ex, resid, gacc, hi, lo, ret,
           stat0, stat1, lall,
           load, e_send, e_recv, f_send, f_recv, w_send, w_recv, m_send, m_recv,
           q_send, q_recv, l_send, l_recv, r_send, r_recv):
    me = lax.axis_index("cls")
    img = lax.axis_index("img")
    grp = lax.axis_index("grp")
    z, x = me // NX, me % NX
    inner = jnp.logical_and(z > 0, z < NZ - 1)
    outer = jnp.logical_not(inner)
    zp = z + 1 - 2 * (z % 2)
    zo = NZ - 1 - z
    zf = NZ - 1 - zp

    def at_chip(sz, sx, core):
        return (grp, sz * NX + sx, core)

    mate = at_chip(z, x, 1 - img)
    side = at_chip(z, 1 - x, img)
    near = at_chip(zp, x, img)
    over = at_chip(zo, x, img)
    others = ((z, 1 - x), (zo, x), (zo, 1 - x))
    peers = [(sz, sx, core) for sz, sx in others for core in (img, 1 - img)] + [(z, x, 1 - img)]

    def rows(at, n):
        return pl.ds(pl.multiple_of(at, 16), n)

    def cols(k, half):
        return pl.ds(pl.multiple_of(k * BOTH + half * CHUNK, CHUNK), CHUNK)

    barrier = pltpu.get_barrier_semaphore()

    def greet(to):
        pl.semaphore_signal(barrier, inc=1, device_id=to, device_id_type=MESH)

    for core in range(2):
        greet(at_chip(zp, x, core))

    @pl.when(outer)
    def _():
        greet(side)

    @pl.when(inner)
    def _():
        for p in peers:
            greet(at_chip(*p))

    def remote(src, dst, sems, to):
        send, recv, at = sems
        return pltpu.make_async_remote_copy(
            src_ref=src, dst_ref=dst, send_sem=send.at[at], recv_sem=recv.at[at],
            device_id=to, device_id_type=MESH)

    def shard(sz, sx, at, n, k):
        return xd.at[rows((sz * NX + sx) * WIDTH + at, n), cols(k, img)]

    def piece(kind, k, sz, sx, at, n, to, own=False):
        place = shard(sz, sx, at, n, k)
        src = x_hbm.at[pl.ds(at, n), pl.ds(k * CHUNK, CHUNK)] if own else place
        return remote(src, place, (e_send, e_recv, (kind, k)), to)

    def change_piece(step, half, j):
        return pltpu.make_async_remote_copy(
            src_ref=ret.at[step, pl.ds(half * FEATS + 256 * j, 256)],
            dst_ref=ret.at[step, pl.ds(256 * j, 256)],
            send_sem=r_send.at[step, half * 3 + j], recv_sem=r_recv.at[step, j],
            device_id=at_chip(zp, x, half), device_id_type=MESH)

    def loss_piece(half):
        place = lall.at[half]
        return pltpu.make_async_remote_copy(
            src_ref=place, dst_ref=place, send_sem=r_send.at[ITERS, half],
            recv_sem=r_recv.at[ITERS, 0], device_id=at_chip(zp, x, half), device_id_type=MESH)

    label_load = pltpu.make_async_copy(lab_hbm, labs.at[img], load.at[6])

    def threshold():
        return 0.16 * jnp.exp2(jnp.full((1, 1), s_ref[0], jnp.int32).astype(jnp.float32))

    def step_to(old, change, lam):
        moved = old - change
        return moved - jnp.clip(moved, -lam, lam)

    def blocks(n, at=0):
        return [slice(at + 256 * j, at + 256 * j + 256) for j in range(n)]

    @pl.when(outer)
    def _():
        def own(k):
            return piece(UP_OWN, k, z, x, 0, WIDTH, near, own=True)

        def cross(part):
            at = (1 - part) * HALF
            places = [
                xd.at[rows((z * NX + sx) * WIDTH + at, HALF), pl.ds(0, IMGS)] for sx in (x, 1 - x)
            ]
            return [
                remote(src, dst, (e_send, e_recv, (ACROSS, part)), side)
                for src, dst in ((x_hbm.at[pl.ds(at, HALF)], places[0]), (places[1], places[1]))
            ]

        def onward(kind, k):
            at = (0, HALF)[kind == UP_FWD]
            r = rows((z * NX + 1 - x) * WIDTH + at, HALF)
            return remote(
                xd.at[r, pl.ds(k * CHUNK, CHUNK)], xd.at[r, cols(k, img)],
                (e_send, e_recv, (kind, k)), near)

        get = pltpu.make_async_copy(w_hbm, master.at[pl.ds(0, FEATS)], load.at[0])
        get.start()
        pl.semaphore_wait(barrier, 3)
        for k in range(CHUNKS):
            own(k).start()
        for part in range(2):
            cross(part)[0].start()
        get.wait()
        w = master[:FEATS]
        top = w.astype(jnp.bfloat16)
        hi[img] = top
        lo[img] = (w - top.astype(jnp.float32)).astype(jnp.bfloat16)

        def probe(buf, k, at, n):
            place = buf.at[img, pl.ds(at, n)]
            return pltpu.make_async_remote_copy(
                src_ref=place, dst_ref=place, send_sem=w_send.at[k], recv_sem=w_recv.at[k, img],
                device_id=at_chip(zp, x, 1), device_id_type=MESH)

        probes = [probe(hi, 0, 0, FEATS)] + [probe(lo, 1 + j, 256 * j, 256) for j in range(3)]
        probes[0].start()
        for part, kind in ((0, UP_FWD), (1, UP_END)):
            cross(part)[1].wait_recv()
            for k in range(CHUNKS):
                onward(kind, k).start()
        for c in probes[1:]:
            c.start()
        lam = threshold()
        for j, r in enumerate(blocks(3)):
            change_piece(0, 0, j).wait_recv()
            master[r] = step_to(master[r], ret[0, r].astype(jnp.float32), lam)
        for k in range(CHUNKS):
            own(k).wait_send()
            onward(UP_FWD, k).wait_send()
            onward(UP_END, k).wait_send()
        for part in range(2):
            cross(part)[0].wait_send()
        for c in probes:
            c.wait_send()
        loss_piece(img).wait_recv()
        loss_ref[...] = lall[img]
        for j, r in enumerate(blocks(3)):
            change_piece(1, 0, j).wait_recv()
            out_ref[r] = step_to(master[r], ret[1, r].astype(jnp.float32), lam)

    @pl.when(inner)
    def _():
        first, second = img == 0, img == 1

        def x_own(k, sx=x, own=True):
            return piece(X_OWN, k, z, sx, 0, WIDTH, side, own)

        def z_own(k, sz=z, own=True):
            return piece(Z_OWN, k, sz, x, 0, WIDTH, over, own)

        def x_mid(k, sx=x):
            return piece(X_MID, k, zo, sx, 0, WIDTH, side)

        def x_far(k, sx=x):
            return piece(X_FAR, k, zf, sx, 0, HALF, side)

        def z_far(k, sz=zp):
            return piece(Z_FAR, k, sz, x, 0, WIDTH, over)

        def z_next(k, sz=zp):
            return piece(Z_NEXT, k, sz, 1 - x, HALF, HALF, over)

        def share(k, sz, sx, at, n, own=False):
            place = shard(sz, sx, at, n, k)
            src = x_hbm.at[pl.ds(at, n), pl.ds(k * CHUNK, CHUNK)] if own else place
            remote(src, place, (f_send, f_recv, k), mate).start()

        def shared(k, half):
            place = xd.at[:, cols(k, half)]
            return remote(place, place, (f_send, f_recv, k), mate)

        def get_own(k):
            return pltpu.make_async_copy(
                x_hbm.at[:, pl.ds(k * CHUNK, CHUNK)], shard(z, x, 0, WIDTH, k), load.at[1 + k])

        def labels_to(half):
            return remote(labs.at[half], labs.at[half], (m_send, m_recv, 0), mate)

        upper = master.at[pl.ds(FEATS, FEATS)]

        def weights_to():
            return remote(w_hbm, upper, (m_send, m_recv, 1), mate)

        def out_to():
            return remote(upper, out_ref, (m_send, m_recv, 2), mate)

        def block_to(block):
            place = wb0.at[pl.ds(block * CLS, CLS)]
            return remote(place, place, (m_send, m_recv, 3), mate)

        def logit_to(k):
            c = pl.ds(k * CHUNK, CHUNK)
            return remote(logit.at[1 - img, :, c], other.at[:, c], (q_send, q_recv, k), mate)

        def probe_from(buf, k, half, at, n):
            place = buf.at[half, pl.ds(at, n)]
            return pltpu.make_async_remote_copy(
                src_ref=place, dst_ref=place, send_sem=w_send.at[k], recv_sem=w_recv.at[k, half],
                device_id=at_chip(zp, x, half), device_id_type=MESH)

        get = pltpu.make_async_copy(w_hbm, master.at[pl.ds(0, FEATS)], load.at[0])

        @pl.when(first)
        def _():
            get.start()

        for k in range(CHUNKS):
            get_own(k).start()
        label_load.start()
        pl.semaphore_wait(barrier, 2 + PEERS)
        for k in range(CHUNKS):
            x_own(k).start()
            z_own(k).start()
        label_load.wait()
        labels_to(img).start()

        @pl.when(second)
        def _():
            weights_to().start()

        for k in range(CHUNKS):
            share(k, z, x, 0, WIDTH, own=True)

        @pl.when(first)
        def _():
            get.wait()
            weights_to().wait_recv()
            for r in blocks(BLOCKS):
                wb0[:CLS, r] = master[r].T.astype(jnp.bfloat16)

            block_to(0).start()

        for k in range(CHUNKS):
            z_own(k, zo, False).wait_recv()
            x_mid(k).start()
            share(k, zo, x, 0, WIDTH)
            piece(UP_OWN, k, zp, x, 0, WIDTH, near).wait_recv()
            z_far(k).start()
            share(k, zp, x, 0, WIDTH)
            x_own(k, 1 - x, False).wait_recv()
            share(k, z, 1 - x, 0, WIDTH)

        @pl.when(second)
        def _():
            for half in range(2):
                probe_from(hi, 0, half, 0, FEATS).wait_recv()
                for j, r in enumerate(blocks(3)):
                    part = hi[half, r].astype(jnp.float32)
                    q = blocks(3, half * FEATS)[j]
                    master[q] = part
                    wb0[CLS:, q] = part.T.astype(jnp.bfloat16)
            block_to(1).start()

        for k in range(CHUNKS):
            z_far(k, zf).wait_recv()
            x_far(k).start()
            share(k, zf, x, 0, WIDTH)
            piece(UP_FWD, k, zp, 1 - x, HALF, HALF, near).wait_recv()
            z_next(k).start()
            share(k, zp, 1 - x, HALF, HALF)
            get_own(k).wait()

        block_to(1 - img).wait_recv()

        def rank(sz, sx, core):
            return ((sz - 1) * NX + sx) * 2 + core

        mine = rank(z, x, img)
        stat = (stat0, stat1)
        first_class = jnp.where(first, me, zp * NX + x) * CLS

        def stat_piece(step, p, i, where):
            at, n = SPLITS[step][p]
            width = (CHUNK, BOTH)[step]
            place = stat[step].at[where, :, pl.ds(at * width, n * width)]
            return remote(place, place, (l_send, l_recv, (step, p, i)), at_chip(*peers[i]))

        def send_stats(step, k):
            for p, (at, n) in enumerate(SPLITS[step]):
                if k == at + n - 1:
                    for i in range(PEERS):
                        stat_piece(step, p, i, mine).start()

        def wait_stats(step, p):
            for i, peer in enumerate(peers):
                stat_piece(step, p, i, rank(*peer)).wait_recv()

        def hot(half, k):
            cls = first_class + lax.broadcasted_iota(jnp.int32, (CLS, CHUNK), 0)
            return labs[half, :, k * CHUNK:k * CHUNK + CHUNK] == cls

        def hot_both(k):
            return jnp.concatenate([hot(half, k) for half in range(2)], axis=1)

        def span(k, n=1):
            return slice(k * BOTH, (k + n) * BOTH)

        def whole(parts):
            top = functools.reduce(jnp.maximum, parts)
            return top + jnp.log(sum(jnp.exp(v - top) for v in parts))

        def grad_slab(r, c):
            return lax.dot_general(
                xd[r, c], resid[:, c], (((1,), (1,)), ((), ())), preferred_element_type=jnp.float32)

        for k in range(CHUNKS):
            x_mid(k, 1 - x).wait_recv()
            piece(UP_END, k, zp, 1 - x, 0, HALF, near).wait_recv()
            x_far(k, 1 - x).wait_recv()
            z_next(k, zf).wait_recv()
            c = slice(k * CHUNK, k * CHUNK + CHUNK)
            logits = jnp.dot(wb0[...], xd[:, cols(k, img)], preferred_element_type=jnp.float32) * SCALE
            top = jnp.max(logits, axis=0, keepdims=True)
            total = jnp.sum(jnp.exp(logits - top), axis=0, keepdims=True)
            stat0[mine, 0:1, c] = top + jnp.log(total)
            send_stats(0, k)
            logit[0, :, c] = logits[:CLS]
            logit[1, :, c] = logits[CLS:]
            logit_to(k).start()
            share(k, zo, 1 - x, 0, WIDTH)
            share(k, zp, 1 - x, 0, HALF)
            share(k, zf, 1 - x, 0, HALF)
            share(k, zf, 1 - x, HALF, HALF)

        def residual(p):
            wait_stats(0, p)
            at, n = SPLITS[0][p]
            for k in range(at, at + n):
                c = slice(k * CHUNK, k * CHUNK + CHUNK)
                logit_to(k).wait_recv()
                for half, values in ((img, logit[img, :, c]), (1 - img, other[:, c])):
                    lse = whole([stat0[2 * chip + half, 0:1, c] for chip in range(4)])
                    wrong = jnp.exp(values - lse) - jnp.where(hot(half, k), 1.0, 0.0)
                    resid[:, cols(k, half)] = wrong.astype(jnp.bfloat16)

        lam = threshold()
        labels_to(1 - img).wait_recv()
        ends = len(SPLITS[0]) - 1
        for p, (at, n) in enumerate(SPLITS[0]):
            residual(p)
            for k in range(at, at + n):
                shared(k, 1 - img).wait_recv()
            if p < ends:
                for r in blocks(BLOCKS):
                    part = grad_slab(r, span(at, n))
                    gacc[r] = part if p == 0 else gacc[r] + part
        for r in blocks(BLOCKS):
            change = (gacc[r] + grad_slab(r, span(*SPLITS[0][ends]))) * (16.0 * SCALE)
            gacc[r] = change
            ret[0, r] = change.astype(jnp.bfloat16)

        @pl.when(second)
        def _():
            for j in range(BLOCKS):
                change_piece(0, j // 3, j % 3).start()
            for j in range(BLOCKS):
                probe_from(lo, 1 + j % 3, j // 3, 256 * (j % 3), 256).wait_recv()
            for half in range(2):
                q = slice(half * FEATS, half * FEATS + FEATS)
                master[q] += lo[half].astype(jnp.float32)

        for r in blocks(BLOCKS):
            new = step_to(master[r], gacc[r], lam)
            master[r] = new
            wb[:, r] = new.T.astype(jnp.bfloat16)

        tops = []
        for k in range(CHUNKS):
            r = span(k)
            logits = jnp.dot(wb[...], xd[:, r], preferred_element_type=jnp.float32) * SCALE
            top = jnp.max(logits, axis=0, keepdims=True)
            e = jnp.exp(logits - top)
            ex[:, r] = e
            stat1[mine, 0:1, r] = top + jnp.log(jnp.sum(e, axis=0, keepdims=True))
            stat1[mine, 1:2, r] = jnp.sum(jnp.where(hot_both(k), logits, 0.0), axis=0, keepdims=True)
            tops.append(top)
            send_stats(1, k)
        ends = len(SPLITS[1]) - 1
        for p, (at, n) in enumerate(SPLITS[1]):
            wait_stats(1, p)
            for k in range(at, at + n):
                r = span(k)
                lse = whole([stat1[m, 0:1, r] for m in range(PEERS + 1)])
                loss = lse - sum(stat1[m, 1:2, r] for m in range(PEERS + 1))
                for i in range(0, BOTH, 128):
                    half, row = i // CHUNK, (k * CHUNK + i % CHUNK) // 128
                    lall[half, row:row + 1, :] = loss[:, i:i + 128]
                prob = ex[:, r] * jnp.exp(tops[k] - lse)
                resid[:, r] = (prob - jnp.where(hot_both(k), 1.0, 0.0)).astype(jnp.bfloat16)
            if p < ends:
                for r in blocks(BLOCKS):
                    part = grad_slab(r, span(at, n))
                    gacc[r] = part if p == 0 else gacc[r] + part
        def last_change(r):
            return (gacc[r] + grad_slab(r, span(*SPLITS[1][ends]))) * (16.0 * SCALE)

        @pl.when(second)
        def _():
            for j, r in enumerate(blocks(BLOCKS)):
                ret[1, r] = last_change(r).astype(jnp.bfloat16)
                change_piece(1, j // 3, j % 3).start()

        @pl.when(first)
        def _():
            for half in range(2):
                loss_piece(half).start()
            for j, r in enumerate(blocks(BLOCKS)):
                new = step_to(master[r], last_change(r), lam)
                if j < 3:
                    out_ref[r] = new
                else:
                    master[r] = new

        loss_ref[...] = lall[img]

        @pl.when(first)
        def _():
            out_to().start()

        @pl.when(second)
        def _():
            out_to().wait_recv()

        for k in range(CHUNKS):
            for c in (x_own(k), z_own(k), x_mid(k), x_far(k), z_far(k), z_next(k)):
                c.wait_send()
            shared(k, img).wait_send()
            logit_to(k).wait_send()
        labels_to(img).wait_send()
        block_to(img).wait_send()

        @pl.when(first)
        def _():
            out_to().wait_send()
            for half in range(2):
                loss_piece(half).wait_send()

        @pl.when(second)
        def _():
            weights_to().wait_send()
            for step in range(ITERS):
                for j in range(BLOCKS):
                    change_piece(step, j // 3, j % 3).wait_send()

        for step in range(ITERS):
            for p in range(len(SPLITS[step])):
                for i in range(PEERS):
                    stat_piece(step, p, i, mine).wait_send()


def store(weights_ref, losses_ref, weights_out, losses_out, flat, sems):
    copies = [
        pltpu.make_async_copy(weights_ref, weights_out, sems.at[0]),
        pltpu.make_async_copy(flat, losses_out, sems.at[1]),
    ]
    copies[0].start()
    for i in range(IMGS // 128):
        flat[pl.ds(128 * i, 128)] = losses_ref[i]
    copies[1].start()
    for c in copies:
        c.wait()


def fused(embeddings, labels, weights, strength):
    vmem = pl.BlockSpec(memory_space=pltpu.VMEM)
    hbm = pl.BlockSpec(memory_space=pl.ANY)
    f32, bf16 = jnp.float32, jnp.bfloat16
    dma = pltpu.SemaphoreType.DMA
    groups = max(len(v) for v in SPLITS)

    def pinned(array):
        return pltpu.with_memory_space_constraint(array, pltpu.HBM)

    new_weights, losses = pl.pallas_call(
        kernel,
        out_shape=(
            pltpu.VMEM((FEATS, CLS), f32),
            pltpu.VMEM((IMGS // 128, 128), f32),
        ),
        in_specs=[hbm, hbm, hbm, pl.BlockSpec(memory_space=pltpu.SMEM)],
        out_specs=(vmem, vmem),
        scratch_shapes=[
            pltpu.VMEM((D, 2 * IMGS), bf16),
            pltpu.VMEM((2, 1, IMGS), jnp.int32),
            pltpu.VMEM((D, CLS), f32),
            pltpu.VMEM((2 * CLS, D), bf16),
            pltpu.VMEM((CLS, D), bf16),
            pltpu.VMEM((2, CLS, IMGS), f32),
            pltpu.VMEM((CLS, IMGS), f32),
            pltpu.VMEM((CLS, 2 * IMGS), f32),
            pltpu.VMEM((CLS, 2 * IMGS), bf16),
            pltpu.VMEM((D, CLS), f32),
            pltpu.VMEM((2, FEATS, CLS), bf16),
            pltpu.VMEM((2, FEATS, CLS), bf16),
            pltpu.VMEM((ITERS, D, CLS), bf16),
            pltpu.VMEM((PEERS + 1, 1, IMGS), f32),
            pltpu.VMEM((PEERS + 1, 2, 2 * IMGS), f32),
            pltpu.VMEM((2, IMGS // 128, 128), f32),
            dma((3 + CHUNKS,)),
            dma((10, CHUNKS)),
            dma((10, CHUNKS)),
            dma((CHUNKS,)),
            dma((CHUNKS,)),
            dma((4,)),
            dma((4, 2)),
            dma((4,)),
            dma((4,)),
            dma((CHUNKS,)),
            dma((CHUNKS,)),
            dma((ITERS, groups, PEERS)),
            dma((ITERS, groups, PEERS)),
            dma((ITERS + 1, BLOCKS)),
            dma((ITERS + 1, BLOCKS)),
        ],
        compiler_params=pltpu.CompilerParams(
            collective_id=0, has_side_effects=True, vmem_limit_bytes=32 * 1024 * 1024
        ),
    )(
        pinned(embeddings.T), pinned(labels.reshape(1, IMGS)), pinned(weights),
        strength,
    )

    def kept(array):
        return pltpu.with_memory_space_constraint(array, pltpu.VMEM)

    return pl.pallas_call(
        store,
        out_shape=(
            jax.ShapeDtypeStruct((FEATS, CLS), f32),
            jax.ShapeDtypeStruct((IMGS,), f32),
        ),
        in_specs=[vmem, vmem],
        out_specs=(hbm, hbm),
        scratch_shapes=[pltpu.VMEM((IMGS,), f32), dma((2,))],
    )(kept(new_weights), kept(losses))


def general(embeddings, labels, weights, strength):
    lam = 16.0 * 0.01 * jnp.exp2(strength[0].astype(jnp.float32))
    full_x = lax.all_gather(embeddings, "cls", axis=1, tiled=True)
    cls_width = weights.shape[1]
    first_class = lax.axis_index("cls") * cls_width
    classes = first_class + lax.iota(jnp.int32, cls_width)
    onehot = (labels[:, None] == classes[None, :]).astype(jnp.float32)
    master = lax.all_gather(weights, "img", axis=0, tiled=True)
    operand = master.astype(jnp.bfloat16)
    losses = jnp.zeros((labels.shape[0],), jnp.float32)
    for step in range(ITERS):
        logits = jnp.dot(full_x, operand, preferred_element_type=jnp.float32) * SCALE
        local_top = jnp.max(logits, axis=1)
        label_term = jnp.sum(logits * onehot, axis=1)
        top = lax.pmax(local_top, "cls")
        total, picked = lax.psum(
            (jnp.sum(jnp.exp(logits - top[:, None]), axis=1), label_term), "cls"
        )
        lse = top + jnp.log(total)
        losses = lse - picked
        resid = (jnp.exp(logits - lse[:, None]) - onehot).astype(jnp.bfloat16)
        grad_local = (
            lax.dot_general(
                full_x, resid, (((0,), (0,)), ((), ())), preferred_element_type=jnp.float32
            )
            * SCALE
        )
        grad = lax.psum(grad_local, "img")
        master = shrink(master, grad, lam)
        operand = master.astype(jnp.bfloat16)
    rows = weights.shape[0]
    new_weights = lax.dynamic_slice_in_dim(master, lax.axis_index("img") * rows, rows, 0)
    return (new_weights, losses)


def solution(mesh):
    placed = (P(("grp", "img"), "cls"), P(("grp", "img")), P(("grp", "img"), "cls"), P("grp"))
    return jax.shard_map(
        fused if mesh.shape["cls"] == N else general,
        mesh=mesh,
        in_specs=placed,
        out_specs=(P(("grp", "img"), "cls"), P(("grp", "img"))),
        check_vma=False,
    )
```

```python
import functools
import math

import jax
import jax.numpy as jnp
from jax import lax
from jax.experimental import pallas as pl
from jax.experimental.pallas import tpu as pltpu
from jax.sharding import PartitionSpec as P

D = 1536
ITERS = 2
MESH = pl.DeviceIdType.MESH
SCALE = 1.0 / math.sqrt(D)

NX, NZ = 2, 4
N = NX * NZ
IMGS, WIDTH, CLS = 1024, 192, 128
HALF = WIDTH // 2
EDGE = NX * WIDTH
FEATS = D // 2
CHUNK = 256
CHUNKS = IMGS // CHUNK
BOTH = 2 * CHUNK
BLOCKS = D // 256
X_OWN, Z_OWN, X_MID, X_FAR, Z_FAR, Z_NEXT, UP_OWN, UP_FWD, UP_END, ACROSS = range(10)
SPLITS = (((0, 2), (2, 1), (3, 1)), ((0, 2), (2, 2)))
PEERS = 7


def shrink(master, grad, lam):
    moved = master - 16.0 * grad
    return jnp.sign(moved) * jnp.maximum(jnp.abs(moved) - lam, 0.0)


def kernel(x_hbm, lab_hbm, w_hbm, s_ref, out_ref, loss_ref,
           xd, labs, master, wb0, wb, logit, other, ex, resid, gacc, hi, lo, ret,
           stat0, stat1, lall,
           load, e_send, e_recv, f_send, f_recv, w_send, w_recv, m_send, m_recv,
           q_send, q_recv, l_send, l_recv, r_send, r_recv):
    me = lax.axis_index("cls")
    img = lax.axis_index("img")
    grp = lax.axis_index("grp")
    z, x = me // NX, me % NX
    inner = jnp.logical_and(z > 0, z < NZ - 1)
    outer = jnp.logical_not(inner)
    zp = z + 1 - 2 * (z % 2)
    zo = NZ - 1 - z
    zf = NZ - 1 - zp

    def at_chip(sz, sx, core):
        return (grp, sz * NX + sx, core)

    mate = at_chip(z, x, 1 - img)
    side = at_chip(z, 1 - x, img)
    near = at_chip(zp, x, img)
    over = at_chip(zo, x, img)
    others = ((z, 1 - x), (zo, x), (zo, 1 - x))
    peers = [(sz, sx, core) for sz, sx in others for core in (img, 1 - img)] + [(z, x, 1 - img)]

    def rows(at, n):
        return pl.ds(pl.multiple_of(at, 16), n)

    def cols(k, half):
        return pl.ds(pl.multiple_of(k * BOTH + half * CHUNK, CHUNK), CHUNK)

    barrier = pltpu.get_barrier_semaphore()

    def greet(to):
        pl.semaphore_signal(barrier, inc=1, device_id=to, device_id_type=MESH)

    for core in range(2):
        greet(at_chip(zp, x, core))

    @pl.when(outer)
    def _():
        greet(side)

    @pl.when(inner)
    def _():
        for p in peers:
            greet(at_chip(*p))

    def remote(src, dst, sems, to):
        send, recv, at = sems
        return pltpu.make_async_remote_copy(
            src_ref=src, dst_ref=dst, send_sem=send.at[at], recv_sem=recv.at[at],
            device_id=to, device_id_type=MESH)

    def shard(sz, sx, at, n, k):
        return xd.at[rows((sz * NX + sx) * WIDTH + at, n), cols(k, img)]

    def piece(kind, k, sz, sx, at, n, to, own=False):
        place = shard(sz, sx, at, n, k)
        src = x_hbm.at[pl.ds(at, n), pl.ds(k * CHUNK, CHUNK)] if own else place
        return remote(src, place, (e_send, e_recv, (kind, k)), to)

    def change_piece(step, half, j):
        return pltpu.make_async_remote_copy(
            src_ref=ret.at[step, pl.ds(half * FEATS + 256 * j, 256)],
            dst_ref=ret.at[step, pl.ds(256 * j, 256)],
            send_sem=r_send.at[step, half * 3 + j], recv_sem=r_recv.at[step, j],
            device_id=at_chip(zp, x, half), device_id_type=MESH)

    def loss_piece(half):
        place = lall.at[half]
        return pltpu.make_async_remote_copy(
            src_ref=place, dst_ref=place, send_sem=r_send.at[ITERS, half],
            recv_sem=r_recv.at[ITERS, 0], device_id=at_chip(zp, x, half), device_id_type=MESH)

    label_load = pltpu.make_async_copy(lab_hbm, labs.at[img], load.at[6])

    def threshold():
        return 0.16 * jnp.exp2(jnp.full((1, 1), s_ref[0], jnp.int32).astype(jnp.float32))

    def step_to(old, change, lam):
        moved = old - change
        return moved - jnp.clip(moved, -lam, lam)

    def blocks(n, at=0):
        return [slice(at + 256 * j, at + 256 * j + 256) for j in range(n)]

    @pl.when(outer)
    def _():
        def own(k):
            return piece(UP_OWN, k, z, x, 0, WIDTH, near, own=True)

        def cross(part):
            at = (1 - part) * HALF
            places = [
                xd.at[rows((z * NX + sx) * WIDTH + at, HALF), pl.ds(0, IMGS)] for sx in (x, 1 - x)
            ]
            return [
                remote(src, dst, (e_send, e_recv, (ACROSS, part)), side)
                for src, dst in ((x_hbm.at[pl.ds(at, HALF)], places[0]), (places[1], places[1]))
            ]

        def onward(kind, k):
            at = (0, HALF)[kind == UP_FWD]
            r = rows((z * NX + 1 - x) * WIDTH + at, HALF)
            return remote(
                xd.at[r, pl.ds(k * CHUNK, CHUNK)], xd.at[r, cols(k, img)],
                (e_send, e_recv, (kind, k)), near)

        get = pltpu.make_async_copy(w_hbm, master.at[pl.ds(0, FEATS)], load.at[0])
        get.start()
        pl.semaphore_wait(barrier, 3)
        for k in range(CHUNKS):
            own(k).start()
        for part in range(2):
            cross(part)[0].start()
        get.wait()
        w = master[:FEATS]
        top = w.astype(jnp.bfloat16)
        hi[img] = top
        lo[img] = (w - top.astype(jnp.float32)).astype(jnp.bfloat16)

        def probe(buf, k, at, n):
            place = buf.at[img, pl.ds(at, n)]
            return pltpu.make_async_remote_copy(
                src_ref=place, dst_ref=place, send_sem=w_send.at[k], recv_sem=w_recv.at[k, img],
                device_id=at_chip(zp, x, 1), device_id_type=MESH)

        probes = [probe(hi, 0, 0, FEATS)] + [probe(lo, 1 + j, 256 * j, 256) for j in range(3)]
        probes[0].start()
        for part, kind in ((0, UP_FWD), (1, UP_END)):
            cross(part)[1].wait_recv()
            for k in range(CHUNKS):
                onward(kind, k).start()
        for c in probes[1:]:
            c.start()
        lam = threshold()
        for j, r in enumerate(blocks(3)):
            change_piece(0, 0, j).wait_recv()
            master[r] = step_to(master[r], ret[0, r].astype(jnp.float32), lam)
        for k in range(CHUNKS):
            own(k).wait_send()
            onward(UP_FWD, k).wait_send()
            onward(UP_END, k).wait_send()
        for part in range(2):
            cross(part)[0].wait_send()
        for c in probes:
            c.wait_send()
        loss_piece(img).wait_recv()
        loss_ref[...] = lall[img]
        for j, r in enumerate(blocks(3)):
            change_piece(1, 0, j).wait_recv()
            out_ref[r] = step_to(master[r], ret[1, r].astype(jnp.float32), lam)

    @pl.when(inner)
    def _():
        first, second = img == 0, img == 1

        def x_own(k, sx=x, own=True):
            return piece(X_OWN, k, z, sx, 0, WIDTH, side, own)

        def z_own(k, sz=z, own=True):
            return piece(Z_OWN, k, sz, x, 0, WIDTH, over, own)

        def x_mid(k, sx=x):
            return piece(X_MID, k, zo, sx, 0, WIDTH, side)

        def x_far(k, sx=x):
            return piece(X_FAR, k, zf, sx, 0, HALF, side)

        def z_far(k, sz=zp):
            return piece(Z_FAR, k, sz, x, 0, WIDTH, over)

        def z_next(k, sz=zp):
            return piece(Z_NEXT, k, sz, 1 - x, HALF, HALF, over)

        def share(k, sz, sx, at, n, own=False):
            place = shard(sz, sx, at, n, k)
            src = x_hbm.at[pl.ds(at, n), pl.ds(k * CHUNK, CHUNK)] if own else place
            remote(src, place, (f_send, f_recv, k), mate).start()

        def shared(k, half):
            place = xd.at[:, cols(k, half)]
            return remote(place, place, (f_send, f_recv, k), mate)

        def get_own(k):
            return pltpu.make_async_copy(
                x_hbm.at[:, pl.ds(k * CHUNK, CHUNK)], shard(z, x, 0, WIDTH, k), load.at[1 + k])

        def labels_to(half):
            return remote(labs.at[half], labs.at[half], (m_send, m_recv, 0), mate)

        upper = master.at[pl.ds(FEATS, FEATS)]

        def weights_to():
            return remote(w_hbm, upper, (m_send, m_recv, 1), mate)

        def out_to():
            return remote(upper, out_ref, (m_send, m_recv, 2), mate)

        def block_to(block):
            place = wb0.at[pl.ds(block * CLS, CLS)]
            return remote(place, place, (m_send, m_recv, 3), mate)

        def logit_to(k):
            c = pl.ds(k * CHUNK, CHUNK)
            return remote(logit.at[1 - img, :, c], other.at[:, c], (q_send, q_recv, k), mate)

        def probe_from(buf, k, half, at, n):
            place = buf.at[half, pl.ds(at, n)]
            return pltpu.make_async_remote_copy(
                src_ref=place, dst_ref=place, send_sem=w_send.at[k], recv_sem=w_recv.at[k, half],
                device_id=at_chip(zp, x, half), device_id_type=MESH)

        get = pltpu.make_async_copy(w_hbm, master.at[pl.ds(0, FEATS)], load.at[0])

        @pl.when(first)
        def _():
            get.start()

        for k in range(CHUNKS):
            get_own(k).start()
        label_load.start()
        pl.semaphore_wait(barrier, 2 + PEERS)
        for k in range(CHUNKS):
            x_own(k).start()
            z_own(k).start()
        label_load.wait()
        labels_to(img).start()

        @pl.when(second)
        def _():
            weights_to().start()

        for k in range(CHUNKS):
            share(k, z, x, 0, WIDTH, own=True)

        @pl.when(first)
        def _():
            get.wait()
            weights_to().wait_recv()
            for r in blocks(BLOCKS):
                wb0[:CLS, r] = master[r].T.astype(jnp.bfloat16)

            block_to(0).start()

        for k in range(CHUNKS):
            z_own(k, zo, False).wait_recv()
            x_mid(k).start()
            share(k, zo, x, 0, WIDTH)
            piece(UP_OWN, k, zp, x, 0, WIDTH, near).wait_recv()
            z_far(k).start()
            share(k, zp, x, 0, WIDTH)
            x_own(k, 1 - x, False).wait_recv()
            share(k, z, 1 - x, 0, WIDTH)

        @pl.when(second)
        def _():
            for half in range(2):
                probe_from(hi, 0, half, 0, FEATS).wait_recv()
                for j, r in enumerate(blocks(3)):
                    part = hi[half, r].astype(jnp.float32)
                    q = blocks(3, half * FEATS)[j]
                    master[q] = part
                    wb0[CLS:, q] = part.T.astype(jnp.bfloat16)
            block_to(1).start()

        for k in range(CHUNKS):
            z_far(k, zf).wait_recv()
            x_far(k).start()
            share(k, zf, x, 0, WIDTH)
            piece(UP_FWD, k, zp, 1 - x, HALF, HALF, near).wait_recv()
            z_next(k).start()
            share(k, zp, 1 - x, HALF, HALF)
            get_own(k).wait()

        block_to(1 - img).wait_recv()

        def rank(sz, sx, core):
            return ((sz - 1) * NX + sx) * 2 + core

        mine = rank(z, x, img)
        stat = (stat0, stat1)
        first_class = jnp.where(first, me, zp * NX + x) * CLS

        def stat_piece(step, p, i, where):
            at, n = SPLITS[step][p]
            width = (CHUNK, BOTH)[step]
            place = stat[step].at[where, :, pl.ds(at * width, n * width)]
            return remote(place, place, (l_send, l_recv, (step, p, i)), at_chip(*peers[i]))

        def send_stats(step, k):
            for p, (at, n) in enumerate(SPLITS[step]):
                if k == at + n - 1:
                    for i in range(PEERS):
                        stat_piece(step, p, i, mine).start()

        def wait_stats(step, p):
            for i, peer in enumerate(peers):
                stat_piece(step, p, i, rank(*peer)).wait_recv()

        def hot(half, k):
            cls = first_class + lax.broadcasted_iota(jnp.int32, (CLS, CHUNK), 0)
            return labs[half, :, k * CHUNK:k * CHUNK + CHUNK] == cls

        def hot_both(k):
            return jnp.concatenate([hot(half, k) for half in range(2)], axis=1)

        def span(k, n=1):
            return slice(k * BOTH, (k + n) * BOTH)

        def whole(parts):
            top = functools.reduce(jnp.maximum, parts)
            return top + jnp.log(sum(jnp.exp(v - top) for v in parts))

        def grad_slab(r, c):
            return lax.dot_general(
                xd[r, c], resid[:, c], (((1,), (1,)), ((), ())), preferred_element_type=jnp.float32)

        def product(a, b):
            return jnp.dot(a, b, preferred_element_type=jnp.float32)

        def ends_of(ref, axis, c):
            low, high = slice(0, EDGE), slice(D - EDGE, D)
            parts = [ref[r, c] if axis == 0 else ref[c, r] for r in (low, high)]
            return jnp.concatenate(parts, axis=axis)

        middle = slice(EDGE, D - EDGE)
        for k in range(CHUNKS):
            x_mid(k, 1 - x).wait_recv()
            known = product(wb0[:, middle], xd[middle, cols(k, img)])
            piece(UP_END, k, zp, 1 - x, 0, HALF, near).wait_recv()
            x_far(k, 1 - x).wait_recv()
            z_next(k, zf).wait_recv()
            c = slice(k * CHUNK, k * CHUNK + CHUNK)
            rest = product(
                ends_of(wb0, 1, slice(None)), ends_of(xd, 0, cols(k, img)))
            logits = (known + rest) * SCALE
            top = jnp.max(logits, axis=0, keepdims=True)
            total = jnp.sum(jnp.exp(logits - top), axis=0, keepdims=True)
            stat0[mine, 0:1, c] = top + jnp.log(total)
            send_stats(0, k)
            logit[0, :, c] = logits[:CLS]
            logit[1, :, c] = logits[CLS:]
            logit_to(k).start()
            share(k, zo, 1 - x, 0, WIDTH)
            share(k, zp, 1 - x, 0, HALF)
            share(k, zf, 1 - x, 0, HALF)
            share(k, zf, 1 - x, HALF, HALF)

        def residual(p):
            wait_stats(0, p)
            at, n = SPLITS[0][p]
            for k in range(at, at + n):
                c = slice(k * CHUNK, k * CHUNK + CHUNK)
                logit_to(k).wait_recv()
                for half, values in ((img, logit[img, :, c]), (1 - img, other[:, c])):
                    lse = whole([stat0[2 * chip + half, 0:1, c] for chip in range(4)])
                    wrong = jnp.exp(values - lse) - jnp.where(hot(half, k), 1.0, 0.0)
                    resid[:, cols(k, half)] = wrong.astype(jnp.bfloat16)

        lam = threshold()
        labels_to(1 - img).wait_recv()
        ends = len(SPLITS[0]) - 1
        for p, (at, n) in enumerate(SPLITS[0]):
            residual(p)
            for k in range(at, at + n):
                shared(k, 1 - img).wait_recv()
            if p < ends:
                for r in blocks(BLOCKS):
                    part = grad_slab(r, span(at, n))
                    gacc[r] = part if p == 0 else gacc[r] + part
        for r in blocks(BLOCKS):
            change = (gacc[r] + grad_slab(r, span(*SPLITS[0][ends]))) * (16.0 * SCALE)
            gacc[r] = change
            ret[0, r] = change.astype(jnp.bfloat16)

        @pl.when(second)
        def _():
            for j in range(BLOCKS):
                change_piece(0, j // 3, j % 3).start()
            for j in range(BLOCKS):
                probe_from(lo, 1 + j % 3, j // 3, 256 * (j % 3), 256).wait_recv()
            for half in range(2):
                q = slice(half * FEATS, half * FEATS + FEATS)
                master[q] += lo[half].astype(jnp.float32)

        for r in blocks(BLOCKS):
            new = step_to(master[r], gacc[r], lam)
            master[r] = new
            wb[:, r] = new.T.astype(jnp.bfloat16)

        tops = []
        for k in range(CHUNKS):
            r = span(k)
            logits = jnp.dot(wb[...], xd[:, r], preferred_element_type=jnp.float32) * SCALE
            top = jnp.max(logits, axis=0, keepdims=True)
            e = jnp.exp(logits - top)
            ex[:, r] = e
            stat1[mine, 0:1, r] = top + jnp.log(jnp.sum(e, axis=0, keepdims=True))
            stat1[mine, 1:2, r] = jnp.sum(jnp.where(hot_both(k), logits, 0.0), axis=0, keepdims=True)
            tops.append(top)
            send_stats(1, k)
        ends = len(SPLITS[1]) - 1
        for p, (at, n) in enumerate(SPLITS[1]):
            wait_stats(1, p)
            for k in range(at, at + n):
                r = span(k)
                lse = whole([stat1[m, 0:1, r] for m in range(PEERS + 1)])
                loss = lse - sum(stat1[m, 1:2, r] for m in range(PEERS + 1))
                for i in range(0, BOTH, 128):
                    half, row = i // CHUNK, (k * CHUNK + i % CHUNK) // 128
                    lall[half, row:row + 1, :] = loss[:, i:i + 128]
                prob = ex[:, r] * jnp.exp(tops[k] - lse)
                resid[:, r] = (prob - jnp.where(hot_both(k), 1.0, 0.0)).astype(jnp.bfloat16)
            if p < ends:
                for r in blocks(BLOCKS):
                    part = grad_slab(r, span(at, n))
                    gacc[r] = part if p == 0 else gacc[r] + part
        def last_change(r):
            return (gacc[r] + grad_slab(r, span(*SPLITS[1][ends]))) * (16.0 * SCALE)

        @pl.when(second)
        def _():
            for j, r in enumerate(blocks(BLOCKS)):
                ret[1, r] = last_change(r).astype(jnp.bfloat16)
                change_piece(1, j // 3, j % 3).start()

        @pl.when(first)
        def _():
            for half in range(2):
                loss_piece(half).start()
            for j, r in enumerate(blocks(BLOCKS)):
                new = step_to(master[r], last_change(r), lam)
                if j < 3:
                    out_ref[r] = new
                else:
                    master[r] = new

        loss_ref[...] = lall[img]

        @pl.when(first)
        def _():
            out_to().start()

        @pl.when(second)
        def _():
            out_to().wait_recv()

        for k in range(CHUNKS):
            for c in (x_own(k), z_own(k), x_mid(k), x_far(k), z_far(k), z_next(k)):
                c.wait_send()
            shared(k, img).wait_send()
            logit_to(k).wait_send()
        labels_to(img).wait_send()
        block_to(img).wait_send()

        @pl.when(first)
        def _():
            out_to().wait_send()
            for half in range(2):
                loss_piece(half).wait_send()

        @pl.when(second)
        def _():
            weights_to().wait_send()
            for step in range(ITERS):
                for j in range(BLOCKS):
                    change_piece(step, j // 3, j % 3).wait_send()

        for step in range(ITERS):
            for p in range(len(SPLITS[step])):
                for i in range(PEERS):
                    stat_piece(step, p, i, mine).wait_send()


def store(weights_ref, losses_ref, weights_out, losses_out, flat, sems):
    copies = [
        pltpu.make_async_copy(weights_ref, weights_out, sems.at[0]),
        pltpu.make_async_copy(flat, losses_out, sems.at[1]),
    ]
    copies[0].start()
    for i in range(IMGS // 128):
        flat[pl.ds(128 * i, 128)] = losses_ref[i]
    copies[1].start()
    for c in copies:
        c.wait()


def fused(embeddings, labels, weights, strength):
    vmem = pl.BlockSpec(memory_space=pltpu.VMEM)
    hbm = pl.BlockSpec(memory_space=pl.ANY)
    f32, bf16 = jnp.float32, jnp.bfloat16
    dma = pltpu.SemaphoreType.DMA
    groups = max(len(v) for v in SPLITS)

    def pinned(array):
        return pltpu.with_memory_space_constraint(array, pltpu.HBM)

    new_weights, losses = pl.pallas_call(
        kernel,
        out_shape=(
            pltpu.VMEM((FEATS, CLS), f32),
            pltpu.VMEM((IMGS // 128, 128), f32),
        ),
        in_specs=[hbm, hbm, hbm, pl.BlockSpec(memory_space=pltpu.SMEM)],
        out_specs=(vmem, vmem),
        scratch_shapes=[
            pltpu.VMEM((D, 2 * IMGS), bf16),
            pltpu.VMEM((2, 1, IMGS), jnp.int32),
            pltpu.VMEM((D, CLS), f32),
            pltpu.VMEM((2 * CLS, D), bf16),
            pltpu.VMEM((CLS, D), bf16),
            pltpu.VMEM((2, CLS, IMGS), f32),
            pltpu.VMEM((CLS, IMGS), f32),
            pltpu.VMEM((CLS, 2 * IMGS), f32),
            pltpu.VMEM((CLS, 2 * IMGS), bf16),
            pltpu.VMEM((D, CLS), f32),
            pltpu.VMEM((2, FEATS, CLS), bf16),
            pltpu.VMEM((2, FEATS, CLS), bf16),
            pltpu.VMEM((ITERS, D, CLS), bf16),
            pltpu.VMEM((PEERS + 1, 1, IMGS), f32),
            pltpu.VMEM((PEERS + 1, 2, 2 * IMGS), f32),
            pltpu.VMEM((2, IMGS // 128, 128), f32),
            dma((3 + CHUNKS,)),
            dma((10, CHUNKS)),
            dma((10, CHUNKS)),
            dma((CHUNKS,)),
            dma((CHUNKS,)),
            dma((4,)),
            dma((4, 2)),
            dma((4,)),
            dma((4,)),
            dma((CHUNKS,)),
            dma((CHUNKS,)),
            dma((ITERS, groups, PEERS)),
            dma((ITERS, groups, PEERS)),
            dma((ITERS + 1, BLOCKS)),
            dma((ITERS + 1, BLOCKS)),
        ],
        compiler_params=pltpu.CompilerParams(
            collective_id=0, has_side_effects=True, vmem_limit_bytes=32 * 1024 * 1024
        ),
    )(
        pinned(embeddings.T), pinned(labels.reshape(1, IMGS)), pinned(weights),
        strength,
    )

    def kept(array):
        return pltpu.with_memory_space_constraint(array, pltpu.VMEM)

    return pl.pallas_call(
        store,
        out_shape=(
            jax.ShapeDtypeStruct((FEATS, CLS), f32),
            jax.ShapeDtypeStruct((IMGS,), f32),
        ),
        in_specs=[vmem, vmem],
        out_specs=(hbm, hbm),
        scratch_shapes=[pltpu.VMEM((IMGS,), f32), dma((2,))],
    )(kept(new_weights), kept(losses))


def general(embeddings, labels, weights, strength):
    lam = 16.0 * 0.01 * jnp.exp2(strength[0].astype(jnp.float32))
    full_x = lax.all_gather(embeddings, "cls", axis=1, tiled=True)
    cls_width = weights.shape[1]
    first_class = lax.axis_index("cls") * cls_width
    classes = first_class + lax.iota(jnp.int32, cls_width)
    onehot = (labels[:, None] == classes[None, :]).astype(jnp.float32)
    master = lax.all_gather(weights, "img", axis=0, tiled=True)
    operand = master.astype(jnp.bfloat16)
    losses = jnp.zeros((labels.shape[0],), jnp.float32)
    for step in range(ITERS):
        logits = jnp.dot(full_x, operand, preferred_element_type=jnp.float32) * SCALE
        local_top = jnp.max(logits, axis=1)
        label_term = jnp.sum(logits * onehot, axis=1)
        top = lax.pmax(local_top, "cls")
        total, picked = lax.psum(
            (jnp.sum(jnp.exp(logits - top[:, None]), axis=1), label_term), "cls"
        )
        lse = top + jnp.log(total)
        losses = lse - picked
        resid = (jnp.exp(logits - lse[:, None]) - onehot).astype(jnp.bfloat16)
        grad_local = (
            lax.dot_general(
                full_x, resid, (((0,), (0,)), ((), ())), preferred_element_type=jnp.float32
            )
            * SCALE
        )
        grad = lax.psum(grad_local, "img")
        master = shrink(master, grad, lam)
        operand = master.astype(jnp.bfloat16)
    rows = weights.shape[0]
    new_weights = lax.dynamic_slice_in_dim(master, lax.axis_index("img") * rows, rows, 0)
    return (new_weights, losses)


def solution(mesh):
    placed = (P(("grp", "img"), "cls"), P(("grp", "img")), P(("grp", "img"), "cls"), P("grp"))
    return jax.shard_map(
        fused if mesh.shape["cls"] == N else general,
        mesh=mesh,
        in_specs=placed,
        out_specs=(P(("grp", "img"), "cls"), P(("grp", "img"))),
        check_vma=False,
    )
```
